32 devices in a mesh: mask: 2 (over x), gx: 16 (over z, y, core).
Axes of the slice: x: 2, y: 2, z: 4, core: 2. Of those that a mesh axis runs over, the one named last changes fastest.
Arguments:
- e_field: float32 [3, 192, 24, 768], P(None, ('mask', 'gx')), parts along dimension 1, may hold values from -6 to 6
- h_field: float32 [3, 192, 24, 768], P(None, ('mask', 'gx')), parts along dimension 1, may hold values from -6 to 6
- polar: float32 [3, 192, 24, 768], P(None, ('mask', 'gx')), parts along dimension 1, may hold values from -6 to 6
- current: float32 [3, 192, 24, 768], P(None, ('mask', 'gx')), parts along dimension 1, may hold values from -6 to 6
- psi_h: float32 [2, 192, 6, 768], P(None, ('mask', 'gx')), parts along dimension 1, may hold values from -6 to 6
- psi_e: float32 [2, 192, 6, 768], P(None, ('mask', 'gx')), parts along dimension 1, may hold values from -6 to 6
- material: int32 [192, 24, 768], P(('mask', 'gx')), parts along dimension 0, may hold values from 0 to 3, as said below
- inv_eps_table: float32 [4], replicated, may hold values from 0.3 to 1
- decay_table: float32 [4], replicated, may hold values from 0.3 to 0.95
- drive_table: float32 [4], replicated, may hold values from 0.1 to 0.5
- strength_table: float32 [4], replicated, may hold values from 0.2 to 1
- spring_table: float32 [4], replicated, may hold values from 0.05 to 1
- orders: int32 [2, 4096], replicated, may hold values from -32 to 31
Outputs:
- e_out: float32 [3, 192, 24, 768], P(None, ('mask', 'gx')), parts along dimension 1
- h_out: float32 [3, 192, 24, 768], P(None, ('mask', 'gx')), parts along dimension 1
- polar_out: float32 [3, 192, 24, 768], P(None, ('mask', 'gx')), parts along dimension 1
- current_out: float32 [3, 192, 24, 768], P(None, ('mask', 'gx')), parts along dimension 1
- psi_h_out: float32 [2, 192, 6, 768], P(None, ('mask', 'gx')), parts along dimension 1
- psi_e_out: float32 [2, 192, 6, 768], P(None, ('mask', 'gx')), parts along dimension 1
- pupil: float32 [4, 8192], P(None, 'mask'), parts along dimension 1
The draws below stay inside these ranges and needn't reach their ends.
There are 2 independent parts, one for each index of `mask`. The reference program is written for one: setup_inputs(seed, part) draws one part's arguments, and reference() takes and returns one part's arrays. A program takes and returns all parts, laid end to end along the dimension named above; an argument that names none is the same for every part. Nothing has to cross between parts.
Inputs may be any that keep to these rules, and one draw needn't show every extreme that they name: `material`: 0 is vacuum, 1 absorber, 2 molybdenum, 3 silicon.
All inputs are finite; a program needn't handle non-finite values.
Results may differ from the reference program's by a relative error of at most 0.000082.
Values sent between devices are 32-bit elements; how exact they have to be, the bound alone decides.
No kernel may reach another device: no remote copies, remote signals or barrier semaphores. Data moves between devices by JAX's collectives and lax.ppermute only.
A program may use at most 64 MiB of HBM per device.

```python
import math
import jax
import jax.numpy as jnp
from jax import lax

NY = 768
NZ = 24
NPML = 6
ABSORB = 6
NMAT = 4
KSPAN = 64
ORDERS = 4096
STEPS = 4
NX = 96


def draw_material(key, part):
    key_pattern, key_thick, key_rough = jax.random.split(key, 3)
    pattern = jax.random.randint(key_pattern, (NX, NY), 0, 2).astype(jnp.int32)
    thick = jax.random.randint(key_thick, (NZ,), 1, 4).astype(jnp.int32)
    bounds = jnp.cumsum(thick)
    rough = jax.random.randint(key_rough, (NX, NY), 0, 2).astype(jnp.int32)
    levels = jnp.arange(NZ + 2, dtype=jnp.int32)
    layer_table = jnp.sum((bounds[None, :] <= levels[:, None]).astype(jnp.int32), axis=1)
    rows = jnp.arange(NZ, dtype=jnp.int32)
    depth = rows - NPML - ABSORB
    shifted = jnp.clip(depth[None, :, None] + rough[:, None, :], 0, NZ + 1)
    layer = jnp.take(layer_table, shifted)
    stack = 2 + layer % 2
    top = jnp.where(rows < NPML, 0, 1)[None, :, None] * pattern[:, None, :]
    result = jnp.where((rows < NPML + ABSORB)[None, :, None], top, stack)
    return result.astype(jnp.int32)


def touch_ends(drawn, stream_key, smallest, high):
    dims = drawn.shape
    spot = [jax.random.randint(jax.random.fold_in(stream_key, axis), (), 0, dims[axis]) for axis in range(len(dims))]
    drawn = drawn.at[tuple(spot)].set(smallest)
    longest = dims.index(max(dims))
    spot[longest] = (spot[longest] + 1) % dims[longest]
    return drawn.at[tuple(spot)].set(high)


def block_levels(stream_key, shape, shards, low, high):
    factor_of = 1.0
    for axis_at, shards_of in shards:
        heights = jax.random.uniform(jax.random.fold_in(jax.random.fold_in(stream_key, 6), axis_at), (shards_of,), jnp.float32, low / len(shards), high / len(shards))
        factor_of = factor_of * jnp.repeat(jnp.exp(heights), shape[axis_at] // shards_of).reshape((-1,) + (1,) * (len(shape) - 1 - axis_at))
    return factor_of


def normal_values(rng, dims, scale, reach, shards=(), held_as=jnp.bfloat16):
    values = scale * jax.random.normal(rng, dims, jnp.float32)
    if shards:
        values = values * block_levels(rng, dims, shards, -0.22, 0.18)
    return jnp.clip(values, -reach, reach).astype(held_as)


def setup_inputs(seed: int = 0, part: int = 0) -> dict:
    streams_of = jax.random.split(jax.random.key(seed), 14)
    part_keys = jax.random.split(jax.random.fold_in(streams_of[13], part), 14)
    return {
        "e_field": normal_values(part_keys[0], (3, NX, NZ, NY), 1.0, 6.0, ((1, 16),), jnp.float32),
        "h_field": normal_values(part_keys[1], (3, NX, NZ, NY), 1.0, 6.0, ((1, 16),), jnp.float32),
        "polar": normal_values(part_keys[2], (3, NX, NZ, NY), 1.0, 6.0, ((1, 16),), jnp.float32),
        "current": normal_values(part_keys[3], (3, NX, NZ, NY), 1.0, 6.0, ((1, 16),), jnp.float32),
        "psi_h": normal_values(part_keys[4], (2, NX, NPML, NY), 1.0, 6.0, ((1, 16),), jnp.float32),
        "psi_e": normal_values(part_keys[5], (2, NX, NPML, NY), 1.0, 6.0, ((1, 16),), jnp.float32),
        "material": draw_material(jax.random.fold_in(jax.random.fold_in(streams_of[13], part), 71), part),
        "inv_eps_table": jnp.clip(jnp.exp(jax.random.uniform(streams_of[7], (NMAT,), jnp.float32, math.log(0.3), math.log(1.0))), 0.3, 1.0),
        "decay_table": jnp.clip(jax.random.uniform(streams_of[8], (NMAT,), jnp.float32, 0.3, 0.95), 0.3, 0.95),
        "drive_table": jnp.clip(jax.random.uniform(streams_of[9], (NMAT,), jnp.float32, 0.1, 0.5), 0.1, 0.5),
        "strength_table": jnp.clip(jax.random.uniform(streams_of[10], (NMAT,), jnp.float32, 0.2, 1.0), 0.2, 1.0),
        "spring_table": jnp.clip(jax.random.uniform(streams_of[11], (NMAT,), jnp.float32, 0.05, 1.0), 0.05, 1.0),
        "orders": touch_ends(jax.random.randint(streams_of[12], (2, ORDERS), 0 - KSPAN // 2, KSPAN // 2), jax.random.fold_in(streams_of[12], 1), 0 - KSPAN // 2, (KSPAN // 2) - 1).astype(jnp.int32),
    }


COURANT = 0.5
SIGMA_MAX = 0.8
PML_ALPHA = 0.05

def z_forward(field):
    after = jnp.concatenate([field[..., 1:, :], jnp.zeros_like(field[..., :1, :])], axis=-2)
    return after - field

def z_backward(field):
    before = jnp.concatenate([jnp.zeros_like(field[..., :1, :]), field[..., :-1, :]], axis=-2)
    return field - before

def y_forward(field):
    return jnp.roll(field, -1, axis=-1) - field

def y_backward(field):
    return field - jnp.roll(field, 1, axis=-1)

def pad_rows(memory, total):
    return jnp.pad(memory, ((0, 0), (0, total - memory.shape[-2]), (0, 0)))

def pml_coefficients(layers, offset):
    depth = (layers - jnp.arange(layers, dtype=jnp.float32) - offset) / layers
    sigma = SIGMA_MAX * depth ** 3
    decay = jnp.exp(-(sigma + PML_ALPHA))
    gain = sigma / (sigma + PML_ALPHA) * (decay - 1.0)
    return (decay[:, None], gain[:, None])

def lookup(material, table):
    total = jnp.zeros(material.shape, table.dtype)
    for index in range(table.shape[0]):
        total = total + jnp.where(material == index, table[index], 0.0)
    return total

def h_update(e_x, e_y, e_z, ey_ahead, ez_ahead, h_x, h_y, h_z, psi_hx, psi_hy, decay, gain):
    layers = psi_hx.shape[-2]
    depth_cells = e_x.shape[-2]
    dey_dz = z_forward(e_y)
    dex_dz = z_forward(e_x)
    psi_hx_new = decay * psi_hx + gain * dey_dz[:, :layers]
    psi_hy_new = decay * psi_hy + gain * dex_dz[:, :layers]
    hx_new = h_x - COURANT * (y_forward(e_z) - dey_dz - pad_rows(psi_hx_new, depth_cells))
    hy_new = h_y - COURANT * (dex_dz + pad_rows(psi_hy_new, depth_cells) - (ez_ahead - e_z))
    hz_new = h_z - COURANT * (ey_ahead - e_y - y_forward(e_x))
    return (hx_new, hy_new, hz_new, psi_hx_new, psi_hy_new)

def e_update(hx_new, hy_new, hz_new, hy_behind, hz_behind, psi_ex, psi_ey, decay, gain, e_field, polar, current, coefs):
    inv_eps, decay_j, drive_j, strength, spring = coefs
    layers = psi_ex.shape[-2]
    depth_cells = hx_new.shape[-2]
    dhy_dz = z_backward(hy_new)
    dhx_dz = z_backward(hx_new)
    psi_ex_new = decay * psi_ex + gain * dhy_dz[:, :layers]
    psi_ey_new = decay * psi_ey + gain * dhx_dz[:, :layers]
    curl_x = y_backward(hz_new) - (dhy_dz + pad_rows(psi_ex_new, depth_cells))
    curl_y = dhx_dz + pad_rows(psi_ey_new, depth_cells) - (hz_new - hz_behind)
    curl_z = hy_new - hy_behind - y_backward(hx_new)
    curl = jnp.stack([curl_x, curl_y, curl_z])
    current_new = decay_j * current + drive_j * (strength * e_field - spring * polar)
    polar_new = polar + current_new
    e_new = e_field + inv_eps * (COURANT * curl - current_new)
    return (e_new, polar_new, current_new, psi_ex_new, psi_ey_new)

def y_table(cells, span):
    rows = jnp.arange(cells, dtype=jnp.int32)
    waves = jnp.arange(span, dtype=jnp.int32) - span // 2
    phase = (rows[:, None] * waves[None, :] % cells).astype(jnp.float32) * (2.0 * math.pi / cells)
    return jnp.concatenate([jnp.cos(phase), jnp.sin(phase)], axis=1)

def x_table(rows, cells, span):
    waves = jnp.arange(span, dtype=jnp.int32) - span // 2
    phase = (rows[:, None] * waves[None, :] % cells).astype(jnp.float32) * (2.0 * math.pi / cells)
    return (jnp.cos(phase), jnp.sin(phase))

def local_spectrum(plane, rows, cells_x, span):
    comps, planes, cells_y = plane.shape
    highest = lax.Precision.HIGHEST
    table = y_table(cells_y, span)
    mixed = jnp.dot(plane.reshape(comps * planes, cells_y), table, precision=highest, preferred_element_type=jnp.float32)
    mixed = mixed.reshape(comps, planes, 2, span)
    real_y = mixed[:, :, 0]
    imag_y = -mixed[:, :, 1]
    cos_x, sin_x = x_table(rows, cells_x, span)
    real = jnp.einsum('cxk,xj->cjk', real_y, cos_x, precision=highest) + jnp.einsum('cxk,xj->cjk', imag_y, sin_x, precision=highest)
    imag = jnp.einsum('cxk,xj->cjk', imag_y, cos_x, precision=highest) - jnp.einsum('cxk,xj->cjk', real_y, sin_x, precision=highest)
    return jnp.stack([real, imag], axis=1)

def pick_orders(spectrum, orders, cells_total):
    span = spectrum.shape[-1]
    flat = spectrum.reshape(4, span * span) / math.sqrt(cells_total)
    index = ((orders[0] + span // 2) * span + (orders[1] + span // 2)).astype(jnp.int32)
    return jnp.take(flat, index, axis=1)

def reference(e_field, h_field, polar, current, psi_h, psi_e, material, inv_eps_table, decay_table, drive_table, strength_table, spring_table, orders):
    coefs = tuple((lookup(material, table) for table in (inv_eps_table, decay_table, drive_table, strength_table, spring_table)))
    decay_h, gain_h = pml_coefficients(NPML, 0.5)
    decay_e, gain_e = pml_coefficients(NPML, 0.0)
    for step in range(STEPS):
        e_x, e_y, e_z = (e_field[0], e_field[1], e_field[2])
        hx_new, hy_new, hz_new, psi_hx, psi_hy = h_update(e_x, e_y, e_z, jnp.roll(e_y, -1, 0), jnp.roll(e_z, -1, 0), h_field[0], h_field[1], h_field[2], psi_h[0], psi_h[1], decay_h, gain_h)
        h_field = jnp.stack([hx_new, hy_new, hz_new])
        psi_h = jnp.stack([psi_hx, psi_hy])
        e_field, polar, current, psi_ex, psi_ey = e_update(hx_new, hy_new, hz_new, jnp.roll(hy_new, 1, 0), jnp.roll(hz_new, 1, 0), psi_e[0], psi_e[1], decay_e, gain_e, e_field, polar, current, coefs)
        psi_e = jnp.stack([psi_ex, psi_ey])
    rows = jnp.arange(NX, dtype=jnp.int32)
    spectrum = local_spectrum(e_field[0:2, :, NPML, :], rows, NX, KSPAN)
    pupil = pick_orders(spectrum, orders, NX * NY)
    return (e_field, h_field, polar, current, psi_h, psi_e, pupil)
```

```python
import math

import jax
import jax.numpy as jnp
import numpy as np
from jax import lax
from jax.experimental import pallas as pl
from jax.experimental.pallas import tpu as pltpu
from jax.sharding import PartitionSpec as P

KSPAN = 64
STEPS = 4

COURANT = 0.5
SIGMA_MAX = 0.8
PML_ALPHA = 0.05

ROWS = 8
LANES = 128
F32 = jnp.float32

HBM = pl.BlockSpec(memory_space=pltpu.HBM)
VMEM = pl.BlockSpec(memory_space=pltpu.VMEM)
SMEM = pl.BlockSpec(memory_space=pltpu.SMEM)


def params():
    return pltpu.CompilerParams(vmem_limit_bytes=24 << 20)


def passed_along(value, steps):
    count = lax.axis_size("gx")
    pairs = [(source, (source + steps) % count) for source in range(count)]
    return lax.ppermute(value, "gx", pairs)


def swapped(value, mask):
    count = lax.axis_size("gx")
    return lax.ppermute(value, "gx", [(source, source ^ mask) for source in range(count)])


def pml(layers, offset, width):
    row = lax.broadcasted_iota(jnp.int32, (ROWS, LANES), 0)
    depth = (layers - row.astype(F32) - offset) / layers
    sigma = SIGMA_MAX * depth * depth * depth
    decay = jnp.exp(-(sigma + PML_ALPHA))
    gain = sigma / (sigma + PML_ALPHA) * (decay - 1.0)
    inside = row < layers
    wide = lambda v: jnp.concatenate([jnp.where(inside, v, 0.0)] * (width // LANES), axis=1)
    return wide(decay), wide(gain)


def tile_of(ref, lead, k):
    return ref[(*lead, slice(ROWS * k, ROWS * k + ROWS), slice(None))]


def put_tile(ref, lead, k, value):
    ref[(*lead, slice(ROWS * k, ROWS * k + ROWS), slice(None))] = value


def row_ids(value):
    return lax.broadcasted_iota(jnp.int32, value.shape, 0)


def z_forward(ref, lead, k, tiles, here):
    if k + 1 < tiles:
        after = ref[(*lead, slice(ROWS * k + 1, ROWS * k + ROWS + 1), slice(None))]
    else:
        after = jnp.where(row_ids(here) < ROWS - 1, pltpu.roll(here, ROWS - 1, 0), 0.0)
    return after - here


def z_backward(ref, lead, k, here):
    if k > 0:
        before = ref[(*lead, slice(ROWS * k - 1, ROWS * k + ROWS - 1), slice(None))]
    else:
        before = jnp.where(row_ids(here) > 0, pltpu.roll(here, 1, 0), 0.0)
    return here - before


def y_forward(value):
    return pltpu.roll(value, value.shape[-1] - 1, 1) - value


def y_backward(value):
    return value - pltpu.roll(value, 1, 1)


def lookup(material, table):
    count = table.shape[0]
    total = jnp.full(material.shape, table[count - 1], F32)
    for index in range(count - 1):
        total = jnp.where(material == index, table[index], total)
    return total


def h_plane(e, h, psi_h, i, tiles, coef, last):
    decay, gain = coef
    for k in range(tiles):
        ex, ey, ez = (tile_of(e, (c, i), k) for c in range(3))
        dey_dz = z_forward(e, (1, i), k, tiles, ey)
        curl = y_forward(ez) - dey_dz
        if k == 0:
            memory = decay * psi_h[0, i] + gain * dey_dz
            psi_h[0, i] = memory
            curl = curl - memory
        put_tile(h, (0, i), k, tile_of(h, (0, i), k) - COURANT * curl)
        if last:
            continue
        dex_dz = z_forward(e, (0, i), k, tiles, ex)
        curl = dex_dz - (tile_of(e, (2, i + 1), k) - ez)
        if k == 0:
            memory = decay * psi_h[1, i] + gain * dex_dz
            psi_h[1, i] = memory
            curl = curl + memory
        put_tile(h, (1, i), k, tile_of(h, (1, i), k) - COURANT * curl)
        curl = tile_of(e, (1, i + 1), k) - ey - y_forward(ex)
        put_tile(h, (2, i), k, tile_of(h, (2, i), k) - COURANT * curl)


def e_plane(e, h, polar, current, psi_e, mats, i, tiles, coef, first=False, last=False):
    inv_eps, decay_j, pull, spring = mats
    decay, gain = coef
    for k in range(tiles):
        hx = tile_of(h, (0, i), k)
        dhx_dz = z_backward(h, (0, i), k, hx)
        old = [tile_of(e, (c, i), k) for c in range(3)]
        curl_y = dhx_dz
        curl_z = -y_backward(hx)
        curl_x = None
        if k == 0:
            memory = decay * psi_e[1, i] + gain * dhx_dz
            psi_e[1, i] = memory
            curl_y = curl_y + memory
        if not last:
            hy, hz = (tile_of(h, (c, i), k) for c in (1, 2))
            dhy_dz = z_backward(h, (1, i), k, hy)
            curl_x = y_backward(hz) - dhy_dz
            if k == 0:
                memory = decay * psi_e[0, i] + gain * dhy_dz
                psi_e[0, i] = memory
                curl_x = curl_x - memory
            curl_y = curl_y - hz
            curl_z = curl_z + hy
        if first:
            curl_y = curl_y - COURANT * old[1]
            curl_z = curl_z - COURANT * old[2]
        else:
            curl_y = curl_y + tile_of(h, (2, i - 1), k)
            curl_z = curl_z - tile_of(h, (1, i - 1), k)
        inv, dec, drv, spr = (tile_of(m, (i,), k) for m in mats)
        for c, curl in enumerate((curl_x, curl_y, curl_z)):
            pol = tile_of(polar, (c, i), k)
            cur = dec * tile_of(current, (c, i), k) + (drv * old[c] - spr * pol)
            put_tile(current, (c, i), k, cur)
            put_tile(polar, (c, i), k, pol + cur)
            change = -cur if curl is None else COURANT * curl - cur
            put_tile(e, (c, i), k, old[c] + inv * change)


def sent_ahead(e, h, psi_hy, put_psi, lead_e, lead_h, k, tiles, coef):
    decay, gain = coef
    ex, ey, ez = (tile_of(e, lead_e(c), k) for c in range(3))
    dex_dz = z_forward(e, lead_e(0), k, tiles, ex)
    curl = dex_dz + ez
    if k == 0:
        memory = decay * psi_hy + gain * dex_dz
        put_psi(memory)
        curl = curl + memory
    part_y = tile_of(h, lead_h(0), k) - COURANT * curl
    part_z = tile_of(h, lead_h(1), k) + COURANT * (ey + y_forward(ex))
    return part_y, part_z


def start_all(copies):
    for copy in copies:
        copy.start()


def wait_all(copies):
    for copy in copies:
        copy.wait()


def first_message(e_field, h_field, psi_h, material, inv_table):
    planes, depth, width = e_field.shape[1:]
    layers = psi_h.shape[2]
    tiles = depth // ROWS
    edge = planes - 1
    probe = layers // ROWS * ROWS

    def body(e_in, h_in, psi_in, mat_in, table, back, ahead, psi_out, e, h, psi, mat, sem):
        wanted = [
            (e_in.at[1, 0], back.at[0:depth]),
            (e_in.at[2, 0], back.at[depth : 2 * depth]),
            (e_in.at[:, edge], e),
            (h_in.at[1:3, edge], h),
            (psi_in.at[1, edge], psi.at[0:layers]),
            (mat_in.at[0, probe : probe + ROWS], mat.at[0]),
            (mat_in.at[edge, probe : probe + ROWS], mat.at[1]),
        ]
        psi[...] = jnp.zeros_like(psi)
        copies = [pltpu.make_async_copy(s, d, sem.at[n]) for n, (s, d) in enumerate(wanted)]
        start_all(copies)
        coef = pml(layers, 0.5, width)
        wait_all(copies)
        back[2 * depth : 2 * depth + ROWS, :] = lookup(mat[0], table)
        ahead[2 * depth : 2 * depth + ROWS, :] = lookup(mat[1], table)

        def put_psi(value):
            psi_out[...] = value

        for k in range(tiles):
            part_y, part_z = sent_ahead(e, h, psi[...], put_psi, lambda c: (c,), lambda c: (c,), k, tiles, coef)
            put_tile(ahead, (), k, part_y)
            put_tile(ahead, (), tiles + k, part_z)

    message = pltpu.VMEM((2 * depth + ROWS, width), F32)
    return pl.pallas_call(
        body,
        name="first_message",
        out_shape=(message, message, pltpu.VMEM((ROWS, width), F32)),
        in_specs=[HBM, HBM, HBM, HBM, SMEM],
        out_specs=(VMEM, VMEM, VMEM),
        scratch_shapes=[
            pltpu.VMEM((3, depth, width), F32),
            pltpu.VMEM((2, depth, width), F32),
            pltpu.VMEM((ROWS, width), F32),
            pltpu.VMEM((2, ROWS, width), jnp.int32),
            pltpu.SemaphoreType.DMA((7,)),
        ],
        compiler_params=params(),
    )(e_field, h_field, psi_h, material, inv_table)


def all_planes(e, h, polar, current, psi_h, psi_e, mats, planes, tiles, coef_h, coef_e):
    h_plane(e, h, psi_h, 0, tiles, coef_h, False)
    e_plane(e, h, polar, current, psi_e, mats, 0, tiles, coef_e, first=True)

    def step(i, carry):
        h_plane(e, h, psi_h, i, tiles, coef_h, False)
        e_plane(e, h, polar, current, psi_e, mats, i, tiles, coef_e)
        return carry

    lax.fori_loop(1, planes - 1, step, 0)
    h_plane(e, h, psi_h, planes - 1, tiles, coef_h, True)
    e_plane(e, h, polar, current, psi_e, mats, planes - 1, tiles, coef_e, last=True)


def state_shapes(planes, depth, width):
    field = pltpu.VMEM((3, planes, depth, width), F32)
    memory = pltpu.VMEM((2, planes, ROWS, width), F32)
    return (field, field, field, field, memory, memory)


def first_interior(fields, memories, material, tables, ahead, psi_edge):
    planes, depth, width = material.shape
    layers = memories[0].shape[2]
    tiles = depth // ROWS
    edge = planes - 1

    def body(e_in, h_in, p_in, c_in, ph_in, pe_in, mat_in, t0, t1, t2, t3, t4, ahead, psi_edge, *rest):
        e, h, polar, current, psi_h, psi_e, inv, dec, drv, spr, mat, sem = rest
        zero = jnp.zeros((ROWS, width), F32)
        for c in range(2):
            for i in range(planes):
                psi_h[c, i] = zero
                psi_e[c, i] = zero
        pairs = [(e_in, e), (h_in, h), (p_in, polar), (c_in, current)]

        def copies(i):
            found = [pltpu.make_async_copy(s.at[:, i], d.at[:, i], sem.at[n, i]) for n, (s, d) in enumerate(pairs)]
            found.append(pltpu.make_async_copy(ph_in.at[:, i], psi_h.at[:, i, 0:layers], sem.at[4, i]))
            found.append(pltpu.make_async_copy(pe_in.at[:, i], psi_e.at[:, i, 0:layers], sem.at[5, i]))
            found.append(pltpu.make_async_copy(mat_in.at[i], mat.at[i], sem.at[6, i]))
            return found

        for i in range(planes):
            start_all(copies(i))
        coef_h = pml(layers, 0.5, width)
        coef_e = pml(layers, 0.0, width)
        mats = (inv, dec, drv, spr)

        def arrive(i):
            wait_all(copies(i))
            for k in range(tiles):
                m = tile_of(mat, (i,), k)
                put_tile(inv, (i,), k, lookup(m, t0))
                put_tile(dec, (i,), k, lookup(m, t1))
                drive = lookup(m, t2)
                put_tile(drv, (i,), k, drive * lookup(m, t3))
                put_tile(spr, (i,), k, drive * lookup(m, t4))

        arrive(0)

        def step(i, carry):
            arrive(i + 1)
            h_plane(e, h, psi_h, i, tiles, coef_h, False)
            return carry

        arrive(1)
        h_plane(e, h, psi_h, 0, tiles, coef_h, False)
        e_plane(e, h, polar, current, psi_e, mats, 0, tiles, coef_e, first=True)

        def step(i, carry):
            arrive(i + 1)
            h_plane(e, h, psi_h, i, tiles, coef_h, False)
            e_plane(e, h, polar, current, psi_e, mats, i, tiles, coef_e)
            return carry

        lax.fori_loop(1, edge, step, 0)
        h_plane(e, h, psi_h, edge, tiles, coef_h, True)
        for k in range(tiles):
            put_tile(h, (1, edge), k, tile_of(ahead, (), k))
            put_tile(h, (2, edge), k, tile_of(ahead, (), tiles + k))
        psi_h[1, edge] = psi_edge[...]
        e_plane(e, h, polar, current, psi_e, mats, edge, tiles, coef_e, last=True)

    coef = pltpu.VMEM((planes, depth, width), F32)
    return pl.pallas_call(
        body,
        name="first_interior",
        out_shape=(*state_shapes(planes, depth, width), coef, coef, coef, coef),
        in_specs=[HBM] * 7 + [SMEM] * 5 + [VMEM, VMEM],
        out_specs=(VMEM,) * 10,
        scratch_shapes=[
            pltpu.VMEM((planes, depth, width), jnp.int32),
            pltpu.SemaphoreType.DMA((7, planes)),
        ],
        compiler_params=params(),
    )(*fields, *memories, material, *tables, ahead, psi_edge)


def interior(state, mats, layers):
    planes, depth, width = state[0].shape[1:]
    tiles = depth // ROWS

    def body(*refs):
        mats_in = refs[6:10]
        e, h, polar, current, psi_h, psi_e = refs[10:16]
        coef_h = pml(layers, 0.5, width)
        coef_e = pml(layers, 0.0, width)
        all_planes(e, h, polar, current, psi_h, psi_e, mats_in, planes, tiles, coef_h, coef_e)

    return pl.pallas_call(
        body,
        name="interior",
        out_shape=state_shapes(planes, depth, width),
        in_specs=[VMEM] * 10,
        out_specs=(VMEM,) * 6,
        input_output_aliases={n: n for n in range(6)},
        compiler_params=params(),
    )(*state, *mats)


def close_edges(e, h, psi_e, inv, from_ahead, from_behind, edge, tiles, coef_e):
    decay, gain = coef_e
    for k in range(tiles):
        half = COURANT * tile_of(inv, (0,), k)
        put_tile(e, (1, 0), k, tile_of(e, (1, 0), k) + half * tile_of(from_behind, (), tiles + k))
        put_tile(e, (2, 0), k, tile_of(e, (2, 0), k) - half * tile_of(from_behind, (), k))
        put_tile(h, (1, edge), k, tile_of(h, (1, edge), k) + COURANT * tile_of(from_ahead, (), tiles + k))
        put_tile(h, (2, edge), k, tile_of(h, (2, edge), k) - COURANT * tile_of(from_ahead, (), k))
    for k in range(tiles):
        hy, hz = (tile_of(h, (c, edge), k) for c in (1, 2))
        dhy_dz = z_backward(h, (1, edge), k, hy)
        curl_x = y_backward(hz) - dhy_dz
        if k == 0:
            memory = decay * psi_e[0, edge] + gain * dhy_dz
            psi_e[0, edge] = memory
            curl_x = curl_x - memory
        half = COURANT * tile_of(inv, (edge,), k)
        put_tile(e, (0, edge), k, tile_of(e, (0, edge), k) + half * curl_x)
        put_tile(e, (1, edge), k, tile_of(e, (1, edge), k) - half * hz)
        put_tile(e, (2, edge), k, tile_of(e, (2, edge), k) + half * hy)


def boundary(state, inv, from_ahead, from_behind, layers):
    e_now, h_now, polar, current, psi_h_now, psi_e_now = state
    planes, depth, width = e_now.shape[1:]
    tiles = depth // ROWS
    edge = planes - 1

    def body(e_in, h_in, ph_in, pe_in, inv, from_ahead, from_behind, e, h, psi_h, psi_e, back, ahead):
        coef_h = pml(layers, 0.5, width)
        coef_e = pml(layers, 0.0, width)
        close_edges(e, h, psi_e, inv, from_ahead, from_behind, edge, tiles, coef_e)

        def put_psi(value):
            psi_h[1, edge] = value

        for k in range(tiles):
            put_tile(back, (), k, tile_of(e, (1, 0), k))
            put_tile(back, (), tiles + k, tile_of(e, (2, 0), k))
            part_y, part_z = sent_ahead(
                e, h, psi_h[1, edge], put_psi, lambda c: (c, edge), lambda c: (c + 1, edge), k, tiles, coef_h
            )
            put_tile(h, (1, edge), k, part_y)
            put_tile(h, (2, edge), k, part_z)
            put_tile(ahead, (), k, part_y)
            put_tile(ahead, (), tiles + k, part_z)

    field, _, _, _, memory, _ = state_shapes(planes, depth, width)
    message = pltpu.VMEM((2 * depth, width), F32)
    e, h, psi_h, psi_e, back, ahead = pl.pallas_call(
        body,
        name="boundary",
        out_shape=(field, field, memory, memory, message, message),
        in_specs=[VMEM] * 7,
        out_specs=(VMEM,) * 6,
        input_output_aliases={0: 0, 1: 1, 2: 2, 3: 3},
        compiler_params=params(),
    )(e_now, h_now, psi_h_now, psi_e_now, inv, from_ahead, from_behind)
    return (e, h, polar, current, psi_h, psi_e), back, ahead


def spectral_rows(planes):
    return -(-(2 * planes + 3) // ROWS) * ROWS


def last_interior(state, mats, back, inv_ahead, inv_behind, table, layers):
    planes, depth, width = state[0].shape[1:]
    tiles = depth // ROWS
    edge = planes - 1
    count = spectral_rows(planes)
    at = layers
    inner = at % ROWS

    def body(*refs):
        mats_in = refs[6:10]
        back, inv_ahead, inv_behind, table = refs[10:14]
        e, h, polar, current, psi_h, psi_e, mixed = refs[14:21]
        e_out, h_out, p_out, c_out, ph_out, pe_out = refs[21:27]
        rows, sem = refs[27:]
        coef_h = pml(layers, 0.5, width)
        coef_e = pml(layers, 0.0, width)
        all_planes(e, h, polar, current, psi_h, psi_e, mats_in, planes, tiles, coef_h, coef_e)
        wanted = [
            (polar, p_out),
            (current, c_out),
            (e.at[:, 1:edge], e_out.at[:, 1:edge]),
            (e.at[0, 0], e_out.at[0, 0]),
            (h.at[:, 0:edge], h_out.at[:, 0:edge]),
            (h.at[0, edge], h_out.at[0, edge]),
            (psi_h.at[:, :, 0:layers], ph_out),
            (psi_e.at[:, 0:edge, 0:layers], pe_out.at[:, 0:edge]),
            (psi_e.at[1, edge, 0:layers], pe_out.at[1, edge]),
        ]
        copies = [pltpu.make_async_copy(s, d, sem.at[n]) for n, (s, d) in enumerate(wanted)]
        start_all(copies)

        def line(ref, lead, z):
            return ref[(*lead, slice(z, z + 1), slice(None))]

        rows[...] = jnp.zeros_like(rows)
        for c in range(2):
            for i in range(edge):
                rows[c * planes + i : c * planes + i + 1, :] = line(e, (c, i), at)
        inv = mats_in[0]
        half = COURANT * line(inv, (edge,), at)
        part_y, part_y_up, part_z = line(h, (1, edge), at), line(h, (1, edge), at - 1), line(h, (2, edge), at)
        rows[edge : edge + 1, :] = line(e, (0, edge), at) + half * (y_backward(part_z) - (part_y - part_y_up))
        rows[planes + edge : planes + edge + 1, :] = line(e, (1, edge), at) - half * part_z
        e_y, e_z, e_z_up = line(back, (), at), line(back, (), depth + at), line(back, (), depth + at - 1)
        quarter = COURANT * COURANT * line(inv_behind, (), inner)
        rows[2 * planes : 2 * planes + 1, :] = -quarter * (y_backward(e_y) + (e_z - e_z_up))
        rows[2 * planes + 1 : 2 * planes + 2, :] = quarter * e_y
        rows[2 * planes + 2 : 2 * planes + 3, :] = COURANT * line(inv_ahead, (), inner) * part_z
        mixed[...] = jnp.dot(rows[...], table[...], precision=lax.Precision.HIGHEST, preferred_element_type=F32)
        wait_all(copies)

    field = jax.ShapeDtypeStruct((3, planes, depth, width), F32)
    memory = jax.ShapeDtypeStruct((2, planes, layers, width), F32)
    found = pl.pallas_call(
        body,
        name="last_interior",
        out_shape=(
            *state_shapes(planes, depth, width),
            pltpu.VMEM((count, table.shape[1]), F32),
            *((field,) * 4),
            memory,
            memory,
        ),
        in_specs=[VMEM] * 14,
        out_specs=(*((VMEM,) * 7), *((HBM,) * 6)),
        input_output_aliases={n: n for n in range(6)},
        scratch_shapes=[pltpu.VMEM((count, width), F32), pltpu.SemaphoreType.DMA((9,))],
        compiler_params=params(),
    )(*state, *mats, back, inv_ahead, inv_behind, table)
    return found[:6], found[6], found[7:]


def last_boundary(state, inv, from_ahead, from_behind, outs, layers):
    e_now, h_now, _, _, _, psi_e_now = state
    planes, depth, width = e_now.shape[1:]
    tiles = depth // ROWS
    edge = planes - 1

    def body(e_in, h_in, pe_in, inv, from_ahead, from_behind, e_hbm, h_hbm, pe_hbm, e, h, psi_e, e_out, h_out, pe_out, sem):
        coef_e = pml(layers, 0.0, width)
        close_edges(e, h, psi_e, inv, from_ahead, from_behind, edge, tiles, coef_e)
        wanted = [
            (e.at[1:3, 0], e_out.at[1:3, 0]),
            (e.at[:, edge], e_out.at[:, edge]),
            (h.at[1:3, edge], h_out.at[1:3, edge]),
            (psi_e.at[0, edge, 0:layers], pe_out.at[0, edge]),
        ]
        copies = [pltpu.make_async_copy(s, d, sem.at[n]) for n, (s, d) in enumerate(wanted)]
        start_all(copies)
        wait_all(copies)

    field, _, _, _, memory, _ = state_shapes(planes, depth, width)
    shape = lambda x: jax.ShapeDtypeStruct(x.shape, x.dtype)
    e_out, h_out, p_out, c_out, ph_out, pe_out = outs
    found = pl.pallas_call(
        body,
        name="last_boundary",
        out_shape=(field, field, memory, shape(e_out), shape(h_out), shape(pe_out)),
        in_specs=[VMEM] * 6 + [HBM] * 3,
        out_specs=(VMEM, VMEM, VMEM, HBM, HBM, HBM),
        input_output_aliases={0: 0, 1: 1, 2: 2, 6: 3, 7: 4, 8: 5},
        scratch_shapes=[pltpu.SemaphoreType.DMA((4,))],
        compiler_params=params(),
    )(e_now, h_now, psi_e_now, inv, from_ahead, from_behind, e_out, h_out, pe_out)
    return (found[3], found[4], p_out, c_out, ph_out, found[5])


def y_table(cells):
    phase = np.arange(cells)[:, None] * (np.arange(KSPAN) - KSPAN // 2)[None, :] % cells
    phase = phase.astype(np.float64) * (2.0 * math.pi / cells)
    return np.concatenate([np.cos(phase), np.sin(phase)], axis=1).astype(np.float32)


def x_table(planes, count):
    rows = spectral_rows(planes)
    cells = planes * count
    comp = np.full(rows, -1)
    shift = np.zeros(rows, np.int64)
    comp[:planes], shift[:planes] = 0, np.arange(planes)
    comp[planes : 2 * planes], shift[planes : 2 * planes] = 1, np.arange(planes)
    comp[2 * planes : 2 * planes + 3] = [0, 1, 1]
    shift[2 * planes : 2 * planes + 3] = [-1, -1, planes]
    x = (np.arange(count)[:, None] * planes + shift[None, :]) % cells
    waves = np.arange(KSPAN) - KSPAN // 2
    phase = (waves[:, None, None] * x[None] % cells).astype(np.float64) * (2.0 * math.pi / cells)
    parts = []
    for c in range(2):
        for wave in (np.cos(phase), np.sin(phase)):
            parts.append(np.where(comp[None, None, :] == c, wave, 0.0).reshape(KSPAN, count * rows))
    return np.concatenate(parts, axis=0).astype(np.float32)


def gathered(block):
    count = lax.axis_size("gx")
    assert count & (count - 1) == 0
    pieces = [block]
    reach = 1
    while reach < count:
        ways = min(4, count // reach)
        held = pieces[0] if len(pieces) == 1 else jnp.concatenate(pieces, axis=0)
        pieces = [held] + [swapped(held, reach * way) for way in range(1, ways)]
        reach *= ways
    return pieces


def pick_orders(pieces, table, orders, cells_total):
    rows = spectral_rows_of = None
    count = lax.axis_size("gx")
    total = sum(piece.shape[0] for piece in pieces)
    rows = total // count
    wide = orders.shape[1]
    chunk = 512 if wide % 512 == 0 else wide
    scale = 1.0 / math.sqrt(cells_total)
    here = jnp.reshape(lax.axis_index("gx"), (1,)).astype(jnp.int32)

    def body(here, *refs):
        held = refs[: len(pieces)]
        table, orders, out, mixed = refs[len(pieces) :]
        at = 0
        for ref in held:
            for n in range(ref.shape[0] // rows):
                slot = jnp.bitwise_xor(here[0], at)
                mixed[pl.ds(pl.multiple_of(slot * rows, rows), rows), :] = ref[n * rows : n * rows + rows, :]
                at += 1
        both = jnp.dot(table[...], mixed[...], precision=lax.Precision.HIGHEST, preferred_element_type=F32)
        parts = []
        for c in range(2):
            cosine = both[2 * c * KSPAN : (2 * c + 1) * KSPAN]
            sine = both[(2 * c + 1) * KSPAN : (2 * c + 2) * KSPAN]
            parts.append((cosine[:, :KSPAN] - sine[:, KSPAN:]) * scale)
            parts.append((cosine[:, KSPAN:] + sine[:, :KSPAN]) * -scale)
        spectrum = jnp.concatenate(parts, axis=0)
        high = spectrum.astype(jnp.bfloat16)
        rest = spectrum - high.astype(F32)
        mid = rest.astype(jnp.bfloat16)
        low = (rest - mid.astype(F32)).astype(jnp.bfloat16)
        split = jnp.concatenate([high, mid, low], axis=1)
        for n in range(wide // chunk):
            span = slice(n * chunk, n * chunk + chunk)
            index_x = orders[0:1, span] + KSPAN // 2
            index_y = orders[1:2, span] + KSPAN // 2
            waves = lax.broadcasted_iota(jnp.int32, (KSPAN, chunk), 0)
            hit_y = (waves == index_y).astype(F32).astype(jnp.bfloat16)
            hit_x = waves == index_x
            hits = jnp.concatenate([hit_y] * 3, axis=0)
            lines = jnp.dot(split, hits, preferred_element_type=F32)
            for q in range(4):
                line = jnp.where(hit_x, lines[q * KSPAN : (q + 1) * KSPAN], 0.0)
                out[q : q + 1, span] = jnp.sum(line, axis=0, keepdims=True)

    return pl.pallas_call(
        body,
        name="pick_orders",
        out_shape=jax.ShapeDtypeStruct((4, wide), F32),
        in_specs=[SMEM] + [VMEM] * (len(pieces) + 2),
        out_specs=VMEM,
        scratch_shapes=[pltpu.VMEM((total, 2 * KSPAN), F32)],
        compiler_params=params(),
    )(here, *pieces, table, orders)


def shards(
    e_field,
    h_field,
    polar,
    current,
    psi_h,
    psi_e,
    material,
    inv_eps_table,
    decay_table,
    drive_table,
    strength_table,
    spring_table,
    orders,
):
    planes, depth, width = material.shape
    layers = psi_h.shape[2]
    count = lax.axis_size("gx")
    tables = (inv_eps_table, decay_table, drive_table, strength_table, spring_table)

    back, ahead, psi_edge = first_message(e_field, h_field, psi_h, material, inv_eps_table)
    from_ahead, from_behind = passed_along(back, -1), passed_along(ahead, 1)
    found = first_interior((e_field, h_field, polar, current), (psi_h, psi_e), material, tables, ahead, psi_edge)
    state, mats = found[:6], found[6:]
    inv_ahead = from_ahead[2 * depth :]
    inv_behind = from_behind[2 * depth :]
    for step in range(1, STEPS):
        state, back, ahead = boundary(state, mats[0], from_ahead, from_behind, layers)
        from_ahead, from_behind = passed_along(back, -1), passed_along(ahead, 1)
        if step < STEPS - 1:
            state = interior(state, mats, layers)
    state, mixed, outs = last_interior(
        state, mats, back, inv_ahead, inv_behind, jnp.asarray(y_table(width)), layers
    )
    pieces = gathered(mixed)
    outs = last_boundary(state, mats[0], from_ahead, from_behind, outs, layers)
    pupil = pick_orders(pieces, jnp.asarray(x_table(planes, count)), orders, planes * count * width)
    return (*outs, pupil)


def solution(mesh):
    split = P(None, ("mask", "gx"), None, None)
    in_specs = (split,) * 6 + (P(("mask", "gx"), None, None),) + (P(),) * 6
    out_specs = (split,) * 6 + (P(None, "mask"),)
    return jax.shard_map(shards, mesh=mesh, in_specs=in_specs, out_specs=out_specs, check_vma=False)
```

```python
import math

import jax
import jax.numpy as jnp
import numpy as np
from jax import lax
from jax.experimental import pallas as pl
from jax.experimental.pallas import tpu as pltpu
from jax.sharding import PartitionSpec as P


KSPAN = 64
STEPS = 4

COURANT = 0.5
SIGMA_MAX = 0.8
PML_ALPHA = 0.05

ROWS = 8
LANES = 128
F32 = jnp.float32

HBM = pl.BlockSpec(memory_space=pltpu.HBM)
VMEM = pl.BlockSpec(memory_space=pltpu.VMEM)
SMEM = pl.BlockSpec(memory_space=pltpu.SMEM)


def params():
    return pltpu.CompilerParams(vmem_limit_bytes=24 << 20)


def in_hbm(value):
    return pltpu.with_memory_space_constraint(value, pltpu.HBM)


def exchanged(near, far):
    count = lax.axis_size("gx")
    assert count % 2 == 0
    odd = range(1, count, 2)
    pairs = [(i, (i + 1) % count) for i in odd] + [((i + 1) % count, i) for i in odd]
    far = lax.ppermute(far, "gx", pairs)
    pairs = [(i, i - 1) for i in odd] + [(i - 1, i) for i in odd]
    near = lax.ppermute(near, "gx", pairs)
    return near, far


def is_odd():
    return lax.rem(lax.axis_index("gx"), 2) == 1


def sort_out(back, ahead, near, far):
    @pl.when(is_odd())
    def _():
        near[...] = back[...]
        far[...] = ahead[...]

    @pl.when(jnp.logical_not(is_odd()))
    def _():
        near[...] = ahead[...]
        far[...] = back[...]


def sort_in(near, far, from_ahead, from_behind):
    @pl.when(is_odd())
    def _():
        from_behind[...] = near[...]
        from_ahead[...] = far[...]

    @pl.when(jnp.logical_not(is_odd()))
    def _():
        from_ahead[...] = near[...]
        from_behind[...] = far[...]


def swapped(value, mask):
    count = lax.axis_size("gx")
    return lax.ppermute(value, "gx", [(source, source ^ mask) for source in range(count)])


def pml(layers, offset, width):
    row = lax.broadcasted_iota(jnp.int32, (ROWS, LANES), 0)
    depth = (layers - row.astype(F32) - offset) / layers
    sigma = SIGMA_MAX * depth * depth * depth
    decay = jnp.exp(-(sigma + PML_ALPHA))
    gain = sigma / (sigma + PML_ALPHA) * (decay - 1.0)
    inside = row < layers
    wide = lambda v: jnp.concatenate([jnp.where(inside, v, 0.0)] * (width // LANES), axis=1)
    return wide(decay), wide(gain)


def tile_of(ref, lead, k):
    return ref[(*lead, slice(ROWS * k, ROWS * k + ROWS), slice(None))]


def put_tile(ref, lead, k, value):
    ref[(*lead, slice(ROWS * k, ROWS * k + ROWS), slice(None))] = value


def row_ids(value):
    return lax.broadcasted_iota(jnp.int32, value.shape, 0)


def z_forward(ref, lead, k, tiles, here):
    if k + 1 < tiles:
        after = ref[(*lead, slice(ROWS * k + 1, ROWS * k + ROWS + 1), slice(None))]
    else:
        after = jnp.where(row_ids(here) < ROWS - 1, pltpu.roll(here, ROWS - 1, 0), 0.0)
    return after - here


def z_backward(ref, lead, k, here):
    if k > 0:
        before = ref[(*lead, slice(ROWS * k - 1, ROWS * k + ROWS - 1), slice(None))]
    else:
        before = jnp.where(row_ids(here) > 0, pltpu.roll(here, 1, 0), 0.0)
    return here - before


def y_forward(value):
    return pltpu.roll(value, value.shape[-1] - 1, 1) - value


def y_backward(value):
    return value - pltpu.roll(value, 1, 1)


def lookup(material, table):
    count = table.shape[0]
    total = jnp.full(material.shape, table[count - 1], F32)
    for index in range(count - 1):
        total = jnp.where(material == index, table[index], total)
    return total


def h_plane(e, h_in, h, psi_h, i, tiles, coef, last):
    decay, gain = coef
    for k in range(tiles):
        ex, ey, ez = (tile_of(e, (c, i), k) for c in range(3))
        dey_dz = z_forward(e, (1, i), k, tiles, ey)
        curl = y_forward(ez) - dey_dz
        if k == 0:
            memory = decay * psi_h[0, i] + gain * dey_dz
            psi_h[0, i] = memory
            curl = curl - memory
        put_tile(h, (0, i), k, tile_of(h_in, (0, i), k) - COURANT * curl)
        if last:
            continue
        dex_dz = z_forward(e, (0, i), k, tiles, ex)
        curl = dex_dz - (tile_of(e, (2, i + 1), k) - ez)
        if k == 0:
            memory = decay * psi_h[1, i] + gain * dex_dz
            psi_h[1, i] = memory
            curl = curl + memory
        put_tile(h, (1, i), k, tile_of(h_in, (1, i), k) - COURANT * curl)
        curl = tile_of(e, (1, i + 1), k) - ey - y_forward(ex)
        put_tile(h, (2, i), k, tile_of(h_in, (2, i), k) - COURANT * curl)


def e_plane(old_state, new_state, h, psi_e, mats, i, tiles, coef, first=False, last=False):
    e_in, polar_in, current_in = old_state
    e, polar, current = new_state
    decay, gain = coef
    for k in range(tiles):
        hx = tile_of(h, (0, i), k)
        dhx_dz = z_backward(h, (0, i), k, hx)
        old = [tile_of(e_in, (c, i), k) for c in range(3)]
        curl_y = dhx_dz
        curl_z = -y_backward(hx)
        curl_x = None
        if k == 0:
            memory = decay * psi_e[1, i] + gain * dhx_dz
            psi_e[1, i] = memory
            curl_y = curl_y + memory
        if not last:
            hy, hz = (tile_of(h, (c, i), k) for c in (1, 2))
            dhy_dz = z_backward(h, (1, i), k, hy)
            curl_x = y_backward(hz) - dhy_dz
            if k == 0:
                memory = decay * psi_e[0, i] + gain * dhy_dz
                psi_e[0, i] = memory
                curl_x = curl_x - memory
            curl_y = curl_y - hz
            curl_z = curl_z + hy
        if first:
            curl_y = curl_y - COURANT * old[1]
            curl_z = curl_z - COURANT * old[2]
        else:
            curl_y = curl_y + tile_of(h, (2, i - 1), k)
            curl_z = curl_z - tile_of(h, (1, i - 1), k)
        inv, dec, drv, spr = (tile_of(m, (i,), k) for m in mats)
        for c, curl in enumerate((curl_x, curl_y, curl_z)):
            pol = tile_of(polar_in, (c, i), k)
            cur = dec * tile_of(current_in, (c, i), k) + (drv * old[c] - spr * pol)
            put_tile(current, (c, i), k, cur)
            put_tile(polar, (c, i), k, pol + cur)
            change = -cur if curl is None else COURANT * curl - cur
            put_tile(e, (c, i), k, old[c] + inv * change)


def sent_ahead(e, h, psi_hy, put_psi, lead_e, lead_h, k, tiles, coef):
    decay, gain = coef
    ex, ey, ez = (tile_of(e, lead_e(c), k) for c in range(3))
    dex_dz = z_forward(e, lead_e(0), k, tiles, ex)
    curl = dex_dz + ez
    if k == 0:
        memory = decay * psi_hy + gain * dex_dz
        put_psi(memory)
        curl = curl + memory
    part_y = tile_of(h, lead_h(0), k) - COURANT * curl
    part_z = tile_of(h, lead_h(1), k) + COURANT * (ey + y_forward(ex))
    return part_y, part_z


def start_all(copies):
    for copy in copies:
        copy.start()


def wait_all(copies):
    for copy in copies:
        copy.wait()


def first_message(e_field, h_field, psi_h, material, inv_table):
    planes, depth, width = e_field.shape[1:]
    layers = psi_h.shape[1]
    tiles = depth // ROWS
    edge = planes - 1
    probe = layers // ROWS * ROWS

    def body(e_in, h_in, psi_in, mat_in, table, near, far, ahead, psi_out, back, e, h, psi_rows, psi, mat, sem):
        wanted = [
            (e_in.at[1, 0], back.at[0:depth]),
            (e_in.at[2, 0], back.at[depth : 2 * depth]),
            (e_in.at[:, edge], e),
            (h_in.at[1:3, edge], h),
            (psi_in.at[edge], psi_rows),
            (mat_in.at[0, probe : probe + ROWS], mat.at[0]),
            (mat_in.at[edge, probe : probe + ROWS], mat.at[1]),
        ]
        copies = [pltpu.make_async_copy(s, d, sem.at[n]) for n, (s, d) in enumerate(wanted)]
        start_all(copies)
        psi[...] = jnp.zeros_like(psi)
        coef = pml(layers, 0.5, width)
        wait_all(copies)
        for z in range(layers):
            psi[z : z + 1, :] = psi_rows[z, 1:2, :]
        back[2 * depth : 2 * depth + ROWS, :] = lookup(mat[0], table)
        ahead[2 * depth : 2 * depth + ROWS, :] = lookup(mat[1], table)

        def put_psi(value):
            psi_out[...] = value

        for k in range(tiles):
            part_y, part_z = sent_ahead(e, h, psi[...], put_psi, lambda c: (c,), lambda c: (c,), k, tiles, coef)
            put_tile(ahead, (), k, part_y)
            put_tile(ahead, (), tiles + k, part_z)
        sort_out(back, ahead, near, far)

    message = pltpu.VMEM((2 * depth + ROWS, width), F32)
    return pl.pallas_call(
        body,
        name="first_message",
        out_shape=(message, message, message, pltpu.VMEM((ROWS, width), F32)),
        in_specs=[HBM, HBM, HBM, HBM, SMEM],
        out_specs=(VMEM, VMEM, VMEM, VMEM),
        scratch_shapes=[
            message,
            pltpu.VMEM((3, depth, width), F32),
            pltpu.VMEM((2, depth, width), F32),
            pltpu.VMEM((layers, 2, width), F32),
            pltpu.VMEM((ROWS, width), F32),
            pltpu.VMEM((2, ROWS, width), jnp.int32),
            pltpu.SemaphoreType.DMA((7,)),
        ],
        compiler_params=params(),
    )(*(in_hbm(x) for x in (e_field, h_field, psi_h, material)), inv_table)


def all_planes(old_state, new_state, h_in, h, psi_h, psi_e, mats, planes, tiles, coef_h, coef_e, ahead=None, arrive=None):
    e = old_state[0]
    edge = planes - 1
    if arrive is not None:
        arrive(0)
    h_plane(e, h_in, h, psi_h, 0, tiles, coef_h, False)
    e_plane(old_state, new_state, h, psi_e, mats, 0, tiles, coef_e, first=True)

    def step(i, carry):
        if arrive is not None:
            arrive(i)
        h_plane(e, h_in, h, psi_h, i, tiles, coef_h, False)
        e_plane(old_state, new_state, h, psi_e, mats, i, tiles, coef_e)
        return carry

    lax.fori_loop(1, edge, step, 0)
    if arrive is not None:
        arrive(edge)
    h_plane(e, h_in, h, psi_h, edge, tiles, coef_h, True)
    if ahead is not None:
        for k in range(tiles):
            put_tile(h, (1, edge), k, tile_of(ahead, (), k))
            put_tile(h, (2, edge), k, tile_of(ahead, (), tiles + k))
    e_plane(old_state, new_state, h, psi_e, mats, edge, tiles, coef_e, last=True)


def state_shapes(planes, depth, width):
    field = pltpu.VMEM((3, planes, depth, width), F32)
    memory = pltpu.VMEM((2, planes, ROWS, width), F32)
    return (field, field, field, field, memory, memory)


def first_interior(fields, memories, material, tables, ahead, psi_edge):
    planes, depth, width = material.shape
    layers = memories[0].shape[1]
    tiles = depth // ROWS
    edge = planes - 1

    def body(e_in, h_in, p_in, c_in, ph_in, pe_in, mat, t0, t1, t2, t3, t4, ahead, psi_edge, *rest):
        e, h, polar, current, psi_h, psi_e, inv, dec, drv, spr = rest
        zero = jnp.zeros((ROWS, width), F32)
        for c in range(2):
            for i in range(planes):
                psi_h[c, i] = zero
                psi_e[c, i] = zero
        coef_h = pml(layers, 0.5, width)
        coef_e = pml(layers, 0.0, width)

        def arrive(i):
            for z in range(layers):
                for c in range(2):
                    psi_h[c, i, z : z + 1, :] = ph_in[i, z, c : c + 1, :]
                    psi_e[c, i, z : z + 1, :] = pe_in[i, z, c : c + 1, :]
            if isinstance(i, int) and i == edge:
                psi_h[1, edge] = psi_edge[...]
            for k in range(tiles):
                m = tile_of(mat, (i,), k)
                put_tile(inv, (i,), k, lookup(m, t0))
                put_tile(dec, (i,), k, lookup(m, t1))
                drive = lookup(m, t2)
                put_tile(drv, (i,), k, drive * lookup(m, t3))
                put_tile(spr, (i,), k, drive * lookup(m, t4))

        old_state, new_state = (e_in, p_in, c_in), (e, polar, current)
        mats = (inv, dec, drv, spr)
        all_planes(
            old_state, new_state, h_in, h, psi_h, psi_e, mats, planes, tiles, coef_h, coef_e, ahead, arrive
        )

    coef = pltpu.VMEM((planes, depth, width), F32)
    return pl.pallas_call(
        body,
        name="first_interior",
        out_shape=(*state_shapes(planes, depth, width), coef, coef, coef, coef),
        in_specs=[VMEM] * 7 + [SMEM] * 5 + [VMEM, VMEM],
        out_specs=(VMEM,) * 10,
        compiler_params=params(),
    )(*fields, *memories, material, *tables, ahead, psi_edge)


def interior(state, mats, layers):
    planes, depth, width = state[0].shape[1:]
    tiles = depth // ROWS

    def body(*refs):
        mats_in = refs[6:10]
        e, h, polar, current, psi_h, psi_e = refs[10:16]
        coef_h = pml(layers, 0.5, width)
        coef_e = pml(layers, 0.0, width)
        now = (e, polar, current)
        all_planes(now, now, h, h, psi_h, psi_e, mats_in, planes, tiles, coef_h, coef_e)

    return pl.pallas_call(
        body,
        name="interior",
        out_shape=state_shapes(planes, depth, width),
        in_specs=[VMEM] * 10,
        out_specs=(VMEM,) * 6,
        input_output_aliases={n: n for n in range(6)},
        compiler_params=params(),
    )(*state, *mats)


def close_edges(e, h, psi_e, inv, from_ahead, from_behind, edge, tiles, coef_e):
    decay, gain = coef_e
    for k in range(tiles):
        half = COURANT * tile_of(inv, (0,), k)
        put_tile(e, (1, 0), k, tile_of(e, (1, 0), k) + half * tile_of(from_behind, (), tiles + k))
        put_tile(e, (2, 0), k, tile_of(e, (2, 0), k) - half * tile_of(from_behind, (), k))
        put_tile(h, (1, edge), k, tile_of(h, (1, edge), k) + COURANT * tile_of(from_ahead, (), tiles + k))
        put_tile(h, (2, edge), k, tile_of(h, (2, edge), k) - COURANT * tile_of(from_ahead, (), k))
    for k in range(tiles):
        hy, hz = (tile_of(h, (c, edge), k) for c in (1, 2))
        dhy_dz = z_backward(h, (1, edge), k, hy)
        curl_x = y_backward(hz) - dhy_dz
        if k == 0:
            memory = decay * psi_e[0, edge] + gain * dhy_dz
            psi_e[0, edge] = memory
            curl_x = curl_x - memory
        half = COURANT * tile_of(inv, (edge,), k)
        put_tile(e, (0, edge), k, tile_of(e, (0, edge), k) + half * curl_x)
        put_tile(e, (1, edge), k, tile_of(e, (1, edge), k) - half * hz)
        put_tile(e, (2, edge), k, tile_of(e, (2, edge), k) + half * hy)


def message_scratch(depth, width):
    message = pltpu.VMEM((2 * depth, width), F32)
    return [message, message]


def boundary(state, inv, near, far, layers):
    e_now, h_now, polar, current, psi_h_now, psi_e_now = state
    planes, depth, width = e_now.shape[1:]
    tiles = depth // ROWS
    edge = planes - 1

    def body(e_in, h_in, ph_in, pe_in, inv, near_in, far_in, e, h, psi_h, psi_e, near, far, back, ahead, behind):
        coef_h = pml(layers, 0.5, width)
        coef_e = pml(layers, 0.0, width)
        sort_in(near_in.at[0 : 2 * depth], far_in.at[0 : 2 * depth], ahead, behind)
        close_edges(e, h, psi_e, inv, ahead, behind, edge, tiles, coef_e)

        def put_psi(value):
            psi_h[1, edge] = value

        for k in range(tiles):
            put_tile(back, (), k, tile_of(e, (1, 0), k))
            put_tile(back, (), tiles + k, tile_of(e, (2, 0), k))
            part_y, part_z = sent_ahead(
                e, h, psi_h[1, edge], put_psi, lambda c: (c, edge), lambda c: (c + 1, edge), k, tiles, coef_h
            )
            put_tile(h, (1, edge), k, part_y)
            put_tile(h, (2, edge), k, part_z)
            put_tile(ahead, (), k, part_y)
            put_tile(ahead, (), tiles + k, part_z)
        sort_out(back, ahead, near, far)

    field, _, _, _, memory, _ = state_shapes(planes, depth, width)
    message = pltpu.VMEM((2 * depth, width), F32)
    e, h, psi_h, psi_e, near, far, back = pl.pallas_call(
        body,
        name="boundary",
        out_shape=(field, field, memory, memory, message, message, message),
        in_specs=[VMEM] * 7,
        out_specs=(VMEM,) * 7,
        input_output_aliases={0: 0, 1: 1, 2: 2, 3: 3},
        scratch_shapes=message_scratch(depth, width),
        compiler_params=params(),
    )(e_now, h_now, psi_h_now, psi_e_now, inv, near, far)
    return (e, h, polar, current, psi_h, psi_e), near, far, back


def spectral_rows(planes):
    return -(-(2 * planes + 3) // ROWS) * ROWS


def last_interior(state, mats, back, inv_near, inv_far, table, layers):
    planes, depth, width = state[0].shape[1:]
    tiles = depth // ROWS
    edge = planes - 1
    count = spectral_rows(planes)
    at = layers
    inner = at % ROWS

    def body(*refs):
        mats_in = refs[6:10]
        back, inv_near, inv_far, table = refs[10:14]
        e, h, polar, current, psi_h, psi_e, mixed = refs[14:21]
        e_out, h_out, p_out, c_out, ph_out, pe_out = refs[21:27]
        rows, inv_ahead, inv_behind, ph_rows, pe_rows, sem = refs[27:]
        sort_in(inv_near, inv_far, inv_ahead, inv_behind)
        coef_h = pml(layers, 0.5, width)
        coef_e = pml(layers, 0.0, width)
        now = (e, polar, current)
        all_planes(now, now, h, h, psi_h, psi_e, mats_in, planes, tiles, coef_h, coef_e)
        for i in range(planes):
            for z in range(layers):
                for c in range(2):
                    ph_rows[i, z, c : c + 1, :] = psi_h[c, i, z : z + 1, :]
                    if i < edge:
                        pe_rows[i, z, c : c + 1, :] = psi_e[c, i, z : z + 1, :]
        wanted = [
            (polar, p_out),
            (current, c_out),
            (e.at[:, 1:edge], e_out.at[:, 1:edge]),
            (e.at[0, 0], e_out.at[0, 0]),
            (h.at[:, 0:edge], h_out.at[:, 0:edge]),
            (h.at[0, edge], h_out.at[0, edge]),
            (ph_rows, ph_out),
            (pe_rows, pe_out.at[0:edge]),
        ]
        copies = [pltpu.make_async_copy(s, d, sem.at[n]) for n, (s, d) in enumerate(wanted)]
        start_all(copies)

        def line(ref, lead, z):
            return ref[(*lead, slice(z, z + 1), slice(None))]

        rows[...] = jnp.zeros_like(rows)
        for c in range(2):
            for i in range(edge):
                rows[c * planes + i : c * planes + i + 1, :] = line(e, (c, i), at)
        inv = mats_in[0]
        half = COURANT * line(inv, (edge,), at)
        part_y, part_y_up, part_z = line(h, (1, edge), at), line(h, (1, edge), at - 1), line(h, (2, edge), at)
        rows[edge : edge + 1, :] = line(e, (0, edge), at) + half * (y_backward(part_z) - (part_y - part_y_up))
        rows[planes + edge : planes + edge + 1, :] = line(e, (1, edge), at) - half * part_z
        e_y, e_z, e_z_up = line(back, (), at), line(back, (), depth + at), line(back, (), depth + at - 1)
        quarter = COURANT * COURANT * line(inv_behind, (), inner)
        rows[2 * planes : 2 * planes + 1, :] = -quarter * (y_backward(e_y) + (e_z - e_z_up))
        rows[2 * planes + 1 : 2 * planes + 2, :] = quarter * e_y
        rows[2 * planes + 2 : 2 * planes + 3, :] = COURANT * line(inv_ahead, (), inner) * part_z
        mixed[...] = jnp.dot(rows[...], table[...], precision=lax.Precision.HIGHEST, preferred_element_type=F32)
        wait_all(copies)

    field = jax.ShapeDtypeStruct((3, planes, depth, width), F32)
    memory = jax.ShapeDtypeStruct((planes, layers, 2, width), F32)
    found = pl.pallas_call(
        body,
        name="last_interior",
        out_shape=(
            *state_shapes(planes, depth, width),
            pltpu.VMEM((count, table.shape[1]), F32),
            *((field,) * 4),
            memory,
            memory,
        ),
        in_specs=[VMEM] * 14,
        out_specs=(*((VMEM,) * 7), *((HBM,) * 6)),
        input_output_aliases={n: n for n in range(6)},
        scratch_shapes=[
            pltpu.VMEM((count, width), F32),
            pltpu.VMEM((ROWS, width), F32),
            pltpu.VMEM((ROWS, width), F32),
            pltpu.VMEM((planes, layers, 2, width), F32),
            pltpu.VMEM((edge, layers, 2, width), F32),
            pltpu.SemaphoreType.DMA((9,)),
        ],
        compiler_params=params(),
    )(*state, *mats, back, inv_near, inv_far, table)
    return found[:6], found[6], found[7:]


def last_boundary(state, inv, near, far, outs, layers):
    e_now, h_now, _, _, _, psi_e_now = state
    planes, depth, width = e_now.shape[1:]
    tiles = depth // ROWS
    edge = planes - 1

    def body(e_in, h_in, pe_in, inv, near, far, e_hbm, h_hbm, pe_hbm, *refs):
        e, h, psi_e, e_out, h_out, pe_out, ahead, behind, rows, sem = refs
        coef_e = pml(layers, 0.0, width)
        sort_in(near, far, ahead, behind)
        close_edges(e, h, psi_e, inv, ahead, behind, edge, tiles, coef_e)
        for z in range(layers):
            for c in range(2):
                rows[z, c : c + 1, :] = psi_e[c, edge, z : z + 1, :]
        wanted = [
            (e.at[1:3, 0], e_out.at[1:3, 0]),
            (e.at[:, edge], e_out.at[:, edge]),
            (h.at[1:3, edge], h_out.at[1:3, edge]),
            (rows, pe_out.at[edge]),
        ]
        copies = [pltpu.make_async_copy(s, d, sem.at[n]) for n, (s, d) in enumerate(wanted)]
        start_all(copies)
        wait_all(copies)

    field, _, _, _, memory, _ = state_shapes(planes, depth, width)
    shape = lambda x: jax.ShapeDtypeStruct(x.shape, x.dtype)
    e_out, h_out, p_out, c_out, ph_out, pe_out = outs
    found = pl.pallas_call(
        body,
        name="last_boundary",
        out_shape=(field, field, memory, shape(e_out), shape(h_out), shape(pe_out)),
        in_specs=[VMEM] * 6 + [HBM] * 3,
        out_specs=(VMEM, VMEM, VMEM, HBM, HBM, HBM),
        input_output_aliases={0: 0, 1: 1, 2: 2, 6: 3, 7: 4, 8: 5},
        scratch_shapes=[
            *message_scratch(depth, width),
            pltpu.VMEM((layers, 2, width), F32),
            pltpu.SemaphoreType.DMA((4,)),
        ],
        compiler_params=params(),
    )(e_now, h_now, psi_e_now, inv, near, far, *(in_hbm(x) for x in (e_out, h_out, pe_out)))
    return (found[3], found[4], p_out, c_out, ph_out, found[5])


def y_table(cells):
    phase = np.arange(cells)[:, None] * (np.arange(KSPAN) - KSPAN // 2)[None, :] % cells
    phase = phase.astype(np.float64) * (2.0 * math.pi / cells)
    return np.concatenate([np.cos(phase), np.sin(phase)], axis=1).astype(np.float32)


def x_table(planes, count):
    rows = spectral_rows(planes)
    cells = planes * count
    comp = np.full(rows, -1)
    shift = np.zeros(rows, np.int64)
    comp[:planes], shift[:planes] = 0, np.arange(planes)
    comp[planes : 2 * planes], shift[planes : 2 * planes] = 1, np.arange(planes)
    comp[2 * planes : 2 * planes + 3] = [0, 1, 1]
    shift[2 * planes : 2 * planes + 3] = [-1, -1, planes]
    x = (np.arange(count)[:, None] * planes + shift[None, :]) % cells
    waves = np.arange(KSPAN) - KSPAN // 2
    phase = (waves[:, None, None] * x[None] % cells).astype(np.float64) * (2.0 * math.pi / cells)
    parts = []
    for c in range(2):
        for wave in (np.cos(phase), np.sin(phase)):
            parts.append(np.where(comp[None, None, :] == c, wave, 0.0).reshape(KSPAN, count * rows))
    return np.concatenate(parts, axis=0).astype(np.float32)


def packed(pieces):
    rows, width = pieces[0].shape

    def body(*refs):
        for n in range(len(pieces)):
            refs[-1][n * rows : n * rows + rows, :] = refs[n][...]

    return pl.pallas_call(
        body,
        name="packed",
        out_shape=pltpu.VMEM((rows * len(pieces), width), F32),
        in_specs=[VMEM] * len(pieces),
        out_specs=VMEM,
        compiler_params=params(),
    )(*pieces)


def gathered(block):
    count = lax.axis_size("gx")
    assert count & (count - 1) == 0
    pieces = [block]
    reach = 1
    while reach < count:
        ways = min(4, count // reach)
        held = pieces[0] if len(pieces) == 1 else packed(pieces)
        pieces = [held] + [swapped(held, reach * way) for way in range(1, ways)]
        reach *= ways
    return pieces


def prepared(orders, table_y, table_x):
    wide = orders.shape[1]
    chunk = 512 if wide % 512 == 0 else wide

    def body(orders_in, y_in, x_in, hit_y, hit_x, table_y, table_x, orders, sem):
        wanted = [(orders_in, orders), (y_in, table_y), (x_in, table_x)]
        copies = [pltpu.make_async_copy(s, d, sem.at[n]) for n, (s, d) in enumerate(wanted)]
        start_all(copies)
        wait_all(copies)
        for n in range(wide // chunk):
            span = slice(n * chunk, n * chunk + chunk)
            waves = lax.broadcasted_iota(jnp.int32, (KSPAN, chunk), 0) - KSPAN // 2
            hit = jnp.where(waves == orders[1:2, span], 1.0, 0.0).astype(jnp.bfloat16)
            for part in range(3):
                hit_y[part * KSPAN : (part + 1) * KSPAN, span] = hit
            hit_x[:, span] = jnp.where(waves == orders[0:1, span], 1.0, 0.0)

    return pl.pallas_call(
        body,
        name="prepared",
        out_shape=(
            pltpu.VMEM((3 * KSPAN, wide), jnp.bfloat16),
            pltpu.VMEM((KSPAN, wide), F32),
            pltpu.VMEM(table_y.shape, F32),
            pltpu.VMEM(table_x.shape, F32),
        ),
        in_specs=[HBM] * 3,
        out_specs=(VMEM,) * 4,
        scratch_shapes=[pltpu.VMEM(orders.shape, jnp.int32), pltpu.SemaphoreType.DMA((3,))],
        compiler_params=params(),
    )(in_hbm(orders), in_hbm(table_y), in_hbm(table_x))


def pick_orders(pieces, table, hit_y, hit_x, cells_total):
    count = lax.axis_size("gx")
    total = sum(piece.shape[0] for piece in pieces)
    rows = total // count
    wide = hit_x.shape[1]
    chunk = 512 if wide % 512 == 0 else wide
    scale = 1.0 / math.sqrt(cells_total)

    def body(*refs):
        held = refs[: len(pieces)]
        table, hit_y, hit_x, out, mixed = refs[len(pieces) :]
        here = lax.axis_index("gx")
        at = 0
        for ref in held:
            for n in range(ref.shape[0] // rows):
                slot = jnp.bitwise_xor(here, at)
                mixed[pl.ds(pl.multiple_of(slot * rows, rows), rows), :] = ref[n * rows : n * rows + rows, :]
                at += 1
        both = jnp.dot(table[...], mixed[...], precision=lax.Precision.HIGHEST, preferred_element_type=F32)
        parts = []
        for c in range(2):
            cosine = both[2 * c * KSPAN : (2 * c + 1) * KSPAN]
            sine = both[(2 * c + 1) * KSPAN : (2 * c + 2) * KSPAN]
            parts.append((cosine[:, :KSPAN] - sine[:, KSPAN:]) * scale)
            parts.append((cosine[:, KSPAN:] + sine[:, :KSPAN]) * -scale)
        spectrum = jnp.concatenate(parts, axis=0)
        high = spectrum.astype(jnp.bfloat16)
        rest = spectrum - high.astype(F32)
        mid = rest.astype(jnp.bfloat16)
        low = (rest - mid.astype(F32)).astype(jnp.bfloat16)
        split = jnp.concatenate([high, mid, low], axis=1)
        for n in range(wide // chunk):
            span = slice(n * chunk, n * chunk + chunk)
            lines = jnp.dot(split, hit_y[:, span], preferred_element_type=F32)
            hit = hit_x[:, span]
            for q in range(4):
                line = lines[q * KSPAN : (q + 1) * KSPAN] * hit
                out[q : q + 1, span] = jnp.sum(line, axis=0, keepdims=True)

    return pl.pallas_call(
        body,
        name="pick_orders",
        out_shape=jax.ShapeDtypeStruct((4, wide), F32),
        in_specs=[VMEM] * (len(pieces) + 3),
        out_specs=VMEM,
        scratch_shapes=[pltpu.VMEM((total, 2 * KSPAN), F32)],
        compiler_params=params(),
    )(*pieces, table, hit_y, hit_x)


def shards(
    e_field,
    h_field,
    polar,
    current,
    psi_h,
    psi_e,
    material,
    inv_eps_table,
    decay_table,
    drive_table,
    strength_table,
    spring_table,
    orders,
):
    planes, depth, width = material.shape
    layers = psi_h.shape[2]
    count = lax.axis_size("gx")
    tables = (inv_eps_table, decay_table, drive_table, strength_table, spring_table)
    psi_h, psi_e = (jnp.transpose(psi, (1, 2, 0, 3)) for psi in (psi_h, psi_e))

    near, far, ahead, psi_edge = first_message(e_field, h_field, psi_h, material, inv_eps_table)
    near, far = exchanged(near, far)
    found = first_interior((e_field, h_field, polar, current), (psi_h, psi_e), material, tables, ahead, psi_edge)
    state, mats = found[:6], found[6:]
    inv_near, inv_far = near[2 * depth :], far[2 * depth :]
    hit_y, hit_x, table_y, table_x = prepared(orders, jnp.asarray(y_table(width)), jnp.asarray(x_table(planes, count)))
    for step in range(1, STEPS):
        state, near, far, back = boundary(state, mats[0], near, far, layers)
        near, far = exchanged(near, far)
        if step < STEPS - 1:
            state = interior(state, mats, layers)
        else:
            state, mixed, outs = last_interior(state, mats, back, inv_near, inv_far, table_y, layers)
    pieces = gathered(mixed)
    outs = last_boundary(state, mats[0], near, far, outs, layers)
    pupil = pick_orders(pieces, table_x, hit_y, hit_x, planes * count * width)
    outs = (*outs[:4], *(jnp.transpose(psi, (2, 0, 1, 3)) for psi in outs[4:]))
    return (*outs, pupil)


def solution(mesh):
    split = P(None, ("mask", "gx"), None, None)
    in_specs = (split,) * 6 + (P(("mask", "gx"), None, None),) + (P(),) * 6
    out_specs = (split,) * 6 + (P(None, "mask"),)
    return jax.shard_map(shards, mesh=mesh, in_specs=in_specs, out_specs=out_specs, check_vma=False)
```

```python
import math

import jax
import jax.numpy as jnp
import numpy as np
from jax import lax
from jax.experimental import pallas as pl
from jax.experimental.pallas import tpu as pltpu
from jax.sharding import PartitionSpec as P


KSPAN = 64

COURANT = 0.5
SIGMA_MAX = 0.8
PML_ALPHA = 0.05

ROWS = 8
LANES = 128
F32 = jnp.float32

HBM = pl.BlockSpec(memory_space=pltpu.HBM)
VMEM = pl.BlockSpec(memory_space=pltpu.VMEM)
SMEM = pl.BlockSpec(memory_space=pltpu.SMEM)


def params():
    return pltpu.CompilerParams(vmem_limit_bytes=24 << 20)


def in_hbm(value):
    return pltpu.with_memory_space_constraint(value, pltpu.HBM)


def exchanged(near, far):
    count = lax.axis_size("gx")
    assert count % 2 == 0
    odd = range(1, count, 2)
    pairs = [(i, (i + 1) % count) for i in odd] + [((i + 1) % count, i) for i in odd]
    far = lax.ppermute(far, "gx", pairs)
    pairs = [(i, i - 1) for i in odd] + [(i - 1, i) for i in odd]
    near = lax.ppermute(near, "gx", pairs)
    return near, far


def is_odd():
    return lax.rem(lax.axis_index("gx"), 2) == 1


def sort_out(back, ahead, near, far):
    @pl.when(is_odd())
    def _():
        near[...] = back[...]
        far[...] = ahead[...]

    @pl.when(jnp.logical_not(is_odd()))
    def _():
        near[...] = ahead[...]
        far[...] = back[...]


def sort_in(near, far, from_ahead, from_behind):
    @pl.when(is_odd())
    def _():
        from_behind[...] = near[...]
        from_ahead[...] = far[...]

    @pl.when(jnp.logical_not(is_odd()))
    def _():
        from_ahead[...] = near[...]
        from_behind[...] = far[...]


def swapped(value, mask):
    count = lax.axis_size("gx")
    return lax.ppermute(value, "gx", [(source, source ^ mask) for source in range(count)])


def pml(layers, offset, width):
    row = lax.broadcasted_iota(jnp.int32, (ROWS, LANES), 0)
    depth = (layers - row.astype(F32) - offset) / layers
    sigma = SIGMA_MAX * depth * depth * depth
    decay = jnp.exp(-(sigma + PML_ALPHA))
    gain = sigma / (sigma + PML_ALPHA) * (decay - 1.0)
    inside = row < layers
    wide = lambda v: jnp.concatenate([jnp.where(inside, v, 0.0)] * (width // LANES), axis=1)
    return wide(decay), wide(gain)


def tile_of(ref, lead, k):
    return ref[(*lead, slice(ROWS * k, ROWS * k + ROWS), slice(None))]


def put_tile(ref, lead, k, value):
    ref[(*lead, slice(ROWS * k, ROWS * k + ROWS), slice(None))] = value


def row_ids(value):
    return lax.broadcasted_iota(jnp.int32, value.shape, 0)


def up(ref, lead, k, tiles, here):
    if k + 1 < tiles:
        return ref[(*lead, slice(ROWS * k + 1, ROWS * k + ROWS + 1), slice(None))]
    return jnp.where(row_ids(here) < ROWS - 1, pltpu.roll(here, ROWS - 1, 0), 0.0)


def down(ref, lead, k, here):
    if k > 0:
        return ref[(*lead, slice(ROWS * k - 1, ROWS * k + ROWS - 1), slice(None))]
    return jnp.where(row_ids(here) > 0, pltpu.roll(here, 1, 0), 0.0)


def y_forward(value):
    return pltpu.roll(value, value.shape[-1] - 1, 1) - value


def y_backward(value):
    return value - pltpu.roll(value, 1, 1)


def lookup(material, table):
    count = table.shape[0]
    total = jnp.full(material.shape, table[count - 1], F32)
    for index in range(count - 1):
        total = jnp.where(material == index, table[index], total)
    return total


def h_values(here, above, ahead, old, psi, coef):
    decay, gain = coef
    ex, ey, ez = here
    dex_dz, dey_dz = above[0] - ex, above[1] - ey
    curl_x = y_forward(ez) - dey_dz
    curl_y = dex_dz + ez
    curl_z = -ey - y_forward(ex)
    memory = None
    if psi is not None:
        memory = (decay * psi[0] + gain * dey_dz, decay * psi[1] + gain * dex_dz)
        curl_x = curl_x - memory[0]
        curl_y = curl_y + memory[1]
    if ahead is not None:
        curl_y = curl_y - ahead[1]
        curl_z = curl_z + ahead[0]
    return tuple(o - COURANT * c for o, c in zip(old, (curl_x, curl_y, curl_z))), memory


def curl_of_h(here, below, behind, psi, coef):
    decay, gain = coef
    hx, hy, hz = here
    dhx_dz, dhy_dz = hx - below[0], hy - below[1]
    curl_x = y_backward(hz) - dhy_dz
    curl_y = dhx_dz - hz
    curl_z = hy - y_backward(hx)
    memory = None
    if psi is not None:
        memory = (decay * psi[0] + gain * dhy_dz, decay * psi[1] + gain * dhx_dz)
        curl_x = curl_x - memory[0]
        curl_y = curl_y + memory[1]
    if behind is not None:
        curl_y = curl_y + behind[1]
        curl_z = curl_z - behind[0]
    return (curl_x, curl_y, curl_z), memory


def material_step(old, curl, pol, cur, mats):
    inv, dec, drv, spr = mats
    cur = dec * cur + (drv * old - spr * pol)
    return old + inv * (COURANT * curl - cur), pol + cur, cur


def response(hy, hz, hy_below, half, gain):
    step = hy - hy_below
    curl_x = y_backward(hz) - step
    memory = None
    if gain is not None:
        memory = gain * step
        curl_x = curl_x - memory
    return (half * curl_x, -half * hz, half * hy), memory


def three(ref, i, k):
    return tuple(tile_of(ref, (c, i), k) for c in range(3))


def h_plane(e, h, psi_h, i, tiles, coef, ahead):
    for k in range(tiles):
        here = three(e, i, k)
        above = tuple(up(e, (c, i), k, tiles, here[c]) for c in range(2))
        psi = (psi_h[0, i], psi_h[1, i]) if k == 0 else None
        new, memory = h_values(here, above, ahead(k), three(h, i, k), psi, coef)
        for c in range(3):
            put_tile(h, (c, i), k, new[c])
        if k == 0:
            psi_h[0, i], psi_h[1, i] = memory


def e_plane(e, h, polar, current, psi_e, mats, i, tiles, coef, behind):
    for k in range(tiles):
        here = three(h, i, k)
        below = tuple(down(h, (c, i), k, here[c]) for c in range(2))
        psi = (psi_e[0, i], psi_e[1, i]) if k == 0 else None
        curl, memory = curl_of_h(here, below, behind(k), psi, coef)
        if k == 0:
            psi_e[0, i], psi_e[1, i] = memory
        values = tuple(tile_of(m, (i,), k) for m in mats)
        for c in range(3):
            found = material_step(
                tile_of(e, (c, i), k), curl[c], tile_of(polar, (c, i), k), tile_of(current, (c, i), k), values
            )
            for ref, value in zip((e, polar, current), found):
                put_tile(ref, (c, i), k, value)


def nothing(k):
    return None


def full_step(state, mats, planes, tiles, coef_h, coef_e, ahead, behind, before=None, after=None):
    e, h, polar, current, psi_h, psi_e = state

    def plane(i, ahead, behind):
        if before is not None:
            before(i)
        h_plane(e, h, psi_h, i, tiles, coef_h, ahead)
        e_plane(e, h, polar, current, psi_e, mats, i, tiles, coef_e, behind)
        if after is not None:
            after(i)

    def next_e(i):
        return lambda k: (tile_of(e, (1, i + 1), k), tile_of(e, (2, i + 1), k))

    def past_h(i):
        return lambda k: (tile_of(h, (1, i - 1), k), tile_of(h, (2, i - 1), k))

    def step(i, carry):
        plane(i, next_e(i), past_h(i))
        return carry

    plane(0, next_e(0), behind)
    lax.fori_loop(1, planes - 1, step, 0)
    plane(planes - 1, ahead, past_h(planes - 1))


def pair_of(ref, row, tiles):
    return lambda k: (tile_of(ref, (), row + k), tile_of(ref, (), row + tiles + k))


def outlook(state, mats, scratch, planes, tiles, coef_h, coef_e, back, ahead):
    e, h, polar, current, psi_h, psi_e = state
    h_first, h_last, h_past, e_last = scratch
    edge = planes - 1
    kept = None
    for k in range(tiles):
        for i in (0, edge - 1, edge):
            here = three(e, i, k)
            above = tuple(up(e, (c, i), k, tiles, here[c]) for c in range(2))
            psi = (psi_h[0, i], psi_h[1, i]) if k == 0 else None
            ey_ez = None if i == edge else (tile_of(e, (1, i + 1), k), tile_of(e, (2, i + 1), k))
            new, memory = h_values(here, above, ey_ez, three(h, i, k), psi, coef_h)
            if i == 0:
                put_tile(back, (), k, here[1])
                put_tile(back, (), tiles + k, here[2])
                for c in range(3):
                    put_tile(h_first, (c,), k, new[c])
            elif i == edge:
                put_tile(ahead, (), k, new[1])
                put_tile(ahead, (), tiles + k, new[2])
                for c in range(3):
                    put_tile(h_last, (c,), k, new[c])
                if k == 0:
                    kept = memory
            else:
                put_tile(h_past, (0,), k, new[1])
                put_tile(h_past, (1,), k, new[2])
    for i, ref in ((edge, h_last), (0, h_first)):
        for k in range(tiles):
            here = tuple(tile_of(ref, (c,), k) for c in range(3))
            below = tuple(down(ref, (c,), k, here[c]) for c in range(2))
            psi = (psi_e[0, i], psi_e[1, i]) if k == 0 else None
            behind = (tile_of(h_past, (0,), k), tile_of(h_past, (1,), k)) if i == edge else None
            curl, _ = curl_of_h(here, below, behind, psi, coef_e)
            values = tuple(tile_of(m, (i,), k) for m in mats)
            for c in range(3):
                new, _, _ = material_step(
                    tile_of(e, (c, i), k), curl[c], tile_of(polar, (c, i), k), tile_of(current, (c, i), k), values
                )
                if i == edge:
                    put_tile(e_last, (c,), k, new)
                elif c > 0:
                    put_tile(back, (), (c + 1) * tiles + k, new)
    for k in range(tiles):
        here = tuple(tile_of(e_last, (c,), k) for c in range(3))
        above = tuple(up(e_last, (c,), k, tiles, here[c]) for c in range(2))
        old = tuple(tile_of(h_last, (c,), k) for c in range(3))
        new, _ = h_values(here, above, None, old, kept if k == 0 else None, coef_h)
        put_tile(ahead, (), 2 * tiles + k, new[1])
        put_tile(ahead, (), 3 * tiles + k, new[2])


def outlook_scratch(depth, width):
    field = pltpu.VMEM((3, depth, width), F32)
    return [field, field, pltpu.VMEM((2, depth, width), F32), field]


def start_all(copies):
    for copy in copies:
        copy.start()


def wait_all(copies):
    for copy in copies:
        copy.wait()


def state_shapes(planes, depth, width):
    field = pltpu.VMEM((3, planes, depth, width), F32)
    memory = pltpu.VMEM((2, planes, ROWS, width), F32)
    return (field, field, field, field, memory, memory)


def fill_mats(mats, material, tables, i, tiles):
    t0, t1, t2, t3, t4 = tables
    inv, dec, drv, spr = mats
    for k in range(tiles):
        m = tile_of(material, (i,), k)
        drive = lookup(m, t2)
        put_tile(inv, (i,), k, lookup(m, t0))
        put_tile(dec, (i,), k, lookup(m, t1))
        put_tile(drv, (i,), k, drive * lookup(m, t3))
        put_tile(spr, (i,), k, drive * lookup(m, t4))


def begin(fields, memories, material, tables):
    planes, depth, width = material.shape
    layers = memories[0].shape[1]
    tiles = depth // ROWS
    edge = planes - 1
    rows = 4 * depth + depth + 2 * ROWS
    order = list(dict.fromkeys([0, edge, edge - 1, 1, *range(planes)]))
    first = order[:4]

    def body(*refs):
        sources, tables_in = refs[:7], refs[7:12]
        state = refs[12:18]
        mat, inv, dec, drv, spr, near, far, back = refs[18:26]
        ahead = refs[26]
        scratch = refs[27:31]
        tables = refs[31:36]
        sem, sem_psi, sem_table = refs[36:39]
        zero = jnp.zeros((ROWS, width), F32)
        for ref in state[4:]:
            for c in range(2):
                for i in range(planes):
                    ref[c, i] = zero

        def copies(i):
            found = [
                pltpu.make_async_copy(sources[n].at[:, i], state[n].at[:, i], sem.at[n, i]) for n in range(4)
            ]
            for n in range(2):
                for c in range(2):
                    source = sources[4 + n].at[i, :, c]
                    target = state[4 + n].at[c, i, 0:layers]
                    found.append(pltpu.make_async_copy(source, target, sem_psi.at[2 * n + c, i]))
            found.append(pltpu.make_async_copy(sources[6].at[i], mat.at[i], sem.at[4, i]))
            return found

        small = [pltpu.make_async_copy(s, d, sem_table.at[n]) for n, (s, d) in enumerate(zip(tables_in, tables))]
        start_all(small)
        for i in order:
            start_all(copies(i))
        coef_h = pml(layers, 0.5, width)
        coef_e = pml(layers, 0.0, width)
        wait_all(small)
        for i in first:
            wait_all(copies(i))
        mats = (inv, dec, drv, spr)
        for i in (0, edge):
            fill_mats(mats, mat, tables, i, tiles)
        outlook(state, mats, scratch, planes, tiles, coef_h, coef_e, back, ahead)
        for i, inner, ref in ((0, 1, back), (edge, edge - 1, ahead)):
            for k in range(tiles):
                put_tile(ref, (), 4 * tiles + k, tile_of(inv, (i,), k))
            put_tile(ref, (), 5 * tiles, lookup(tile_of(mat, (inner,), 0), tables[0]))
            put_tile(ref, (), 5 * tiles + 1, tile_of(drv, (i,), 0))
        sort_out(back, ahead, near, far)
        for i in order[4:]:
            wait_all(copies(i))

    message = pltpu.VMEM((rows, width), F32)
    coef = pltpu.VMEM((planes, depth, width), F32)
    found = pl.pallas_call(
        body,
        name="begin",
        out_shape=(
            *state_shapes(planes, depth, width),
            pltpu.VMEM((planes, depth, width), jnp.int32),
            coef,
            coef,
            coef,
            coef,
            message,
            message,
            message,
        ),
        in_specs=[HBM] * 12,
        out_specs=(VMEM,) * 14,
        scratch_shapes=[
            message,
            *outlook_scratch(depth, width),
            *(pltpu.SMEM(table.shape, F32) for table in tables),
            pltpu.SemaphoreType.DMA((5, planes)),
            pltpu.SemaphoreType.DMA((4, planes)),
            pltpu.SemaphoreType.DMA((len(tables),)),
        ],
        compiler_params=params(),
    )(*(in_hbm(x) for x in (*fields, *memories, material, *tables)))
    return found[:6], found[6], found[7:11], found[11], found[12], found[13]


def interior(state, mats, layers, material=None, tables=()):
    planes, depth, width = state[0].shape[1:]
    tiles = depth // ROWS
    fill = material is not None
    extra = (material, *tables) if fill else ()
    count = 10 if fill else 6

    def body(*refs):
        inputs, outputs = refs[: 10 + len(extra)], refs[10 + len(extra) :]
        state = outputs[:6]
        mats = outputs[6:10] if fill else inputs[6:10]
        coef_h = pml(layers, 0.5, width)
        coef_e = pml(layers, 0.0, width)
        if fill:

            def step(i, carry):
                fill_mats(mats, inputs[10], inputs[11:], i, tiles)
                return carry

            lax.fori_loop(1, planes - 1, step, 0)
        full_step(state, mats, planes, tiles, coef_h, coef_e, nothing, nothing)

    coef = pltpu.VMEM((planes, depth, width), F32)
    shapes = (*state_shapes(planes, depth, width), coef, coef, coef, coef)
    found = pl.pallas_call(
        body,
        name="first_interior" if fill else "interior",
        out_shape=shapes[:count],
        in_specs=[VMEM] * 10 + ([VMEM] + [SMEM] * len(tables) if fill else []),
        out_specs=(VMEM,) * count,
        input_output_aliases={n: n for n in range(count)},
        compiler_params=params(),
    )(*state, *mats, *extra)
    return found[:6], (found[6:] if fill else mats)


def close_step(state, mats, back, ahead, behind, around, scratch, planes, tiles, coef_h, coef_e):
    e, h, _, _, _, psi_e = state
    inv = mats[0]
    e_ahead, h_behind, e_turn = scratch
    edge = planes - 1
    gain_h, gain_e = coef_h[1], coef_e[1]
    for k in range(tiles):
        old_y, old_z = tile_of(back, (), k), tile_of(back, (), tiles + k)
        half = COURANT * tile_of(inv, (0,), k)
        hy = tile_of(behind, (), k) + COURANT * old_z
        hz = tile_of(behind, (), tiles + k) - COURANT * old_y
        put_tile(e, (1, 0), k, tile_of(e, (1, 0), k) + half * hz)
        put_tile(e, (2, 0), k, tile_of(e, (2, 0), k) - half * hy)

        far_y, far_z = tile_of(ahead, (), k), tile_of(ahead, (), tiles + k)
        delta_y, delta_z = COURANT * far_z, -COURANT * far_y
        below = COURANT * down(ahead, (), tiles + k, far_z) if k > 0 else down(None, (), 0, delta_y)
        change, memory = response(delta_y, delta_z, below, COURANT * tile_of(inv, (edge,), k), gain_e if k == 0 else None)
        if k == 0:
            psi_e[0, edge] = psi_e[0, edge] + memory
        for c in range(3):
            put_tile(e, (c, edge), k, tile_of(e, (c, edge), k) + change[c])
        hy = tile_of(h, (1, edge), k) + delta_y
        hz = tile_of(h, (2, edge), k) + delta_z
        put_tile(h, (1, edge), k, hy)
        put_tile(h, (2, edge), k, hz)
        half = COURANT * tile_of(around, (), k)
        put_tile(e_ahead, (), k, tile_of(ahead, (), 2 * tiles + k) + half * hz)
        put_tile(e_ahead, (), tiles + k, tile_of(ahead, (), 3 * tiles + k) - half * hy)

        delta_y, delta_z = COURANT * old_z, -COURANT * old_y
        below = COURANT * down(back, (), tiles + k, old_z) if k > 0 else down(None, (), 0, delta_y)
        half = COURANT * tile_of(around, (), tiles + k)
        change, _ = response(delta_y, delta_z, below, half, gain_e if k == 0 else None)
        for c in range(3):
            put_tile(e_turn, (c,), k, change[c])
    for k in range(tiles):
        ex, ey, ez = (tile_of(e_turn, (c,), k) for c in range(3))
        dex_dz = up(e_turn, (0,), k, tiles, ex) - ex
        curl_y = dex_dz + ez
        if k == 0:
            curl_y = curl_y + gain_h * dex_dz
        old_y, old_z = tile_of(back, (), k), tile_of(back, (), tiles + k)
        hy = tile_of(behind, (), 2 * tiles + k) + COURANT * (old_z - curl_y + tile_of(e, (2, 0), k))
        hz = tile_of(behind, (), 3 * tiles + k) + COURANT * (ey + y_forward(ex) - old_y - tile_of(e, (1, 0), k))
        put_tile(h_behind, (), k, hy)
        put_tile(h_behind, (), tiles + k, hz)


def close_scratch(depth, width):
    return [
        pltpu.VMEM((2 * depth, width), F32),
        pltpu.VMEM((2 * depth, width), F32),
        pltpu.VMEM((3, depth, width), F32),
    ]


def middle(state, mats, back, near, far, layers):
    planes, depth, width = state[0].shape[1:]
    tiles = depth // ROWS
    rows = 2 * depth + 4 * ROWS

    def body(*refs):
        mats, back_in, near_in, far_in = refs[6:10], refs[10], refs[11], refs[12]
        state = refs[13:19]
        near, far, back, around = refs[19:23]
        ahead, behind = refs[23:25]
        scratch, outlook_refs, sent = refs[25:28], refs[28:32], refs[32]
        coef_h = pml(layers, 0.5, width)
        coef_e = pml(layers, 0.0, width)
        sort_in(near_in, far_in, ahead, behind)
        for n, ref in enumerate((ahead, behind)):
            for k in range(tiles):
                put_tile(around, (), n * tiles + k, tile_of(ref, (), 4 * tiles + k))
            for k in range(2):
                put_tile(around, (), 2 * tiles + 2 * n + k, tile_of(ref, (), 5 * tiles + k))
        close_step(state, mats, back_in, ahead, behind, around, scratch, planes, tiles, coef_h, coef_e)
        full_step(
            state, mats, planes, tiles, coef_h, coef_e, pair_of(scratch[0], 0, tiles), pair_of(scratch[1], 0, tiles)
        )
        outlook(state, mats, outlook_refs, planes, tiles, coef_h, coef_e, back, sent)
        sort_out(back, sent, near, far)

    message = pltpu.VMEM((4 * depth, width), F32)
    whole = pltpu.VMEM(near.shape, F32)
    found = pl.pallas_call(
        body,
        name="middle",
        out_shape=(*state_shapes(planes, depth, width), message, message, message, pltpu.VMEM((rows, width), F32)),
        in_specs=[VMEM] * 13,
        out_specs=(VMEM,) * 10,
        input_output_aliases={n: n for n in range(6)},
        scratch_shapes=[whole, whole, *close_scratch(depth, width), *outlook_scratch(depth, width), message],
        compiler_params=params(),
    )(*state, *mats, back, near, far)
    return found[:6], found[6], found[7], found[8], found[9]


def spectral_rows(planes):
    return -(-(2 * planes + 7) // ROWS) * ROWS


def foretold(state, mats, around, table, layers):
    planes, depth, width = state[0].shape[1:]
    tiles = depth // ROWS
    edge = planes - 1
    wide = planes + 4
    count = spectral_rows(planes)
    assert 2 <= layers <= ROWS - 2

    def body(*refs):
        mats, around, table = refs[6:10], refs[10], refs[11]
        e, h, polar, current, psi_h, psi_e = refs[12:18]
        mixed, e_one, h_one, p_one, c_one, psi_one, h_two, rows = refs[18:]
        coef_h = pml(layers, 0.5, width)
        coef_e = pml(layers, 0.0, width)
        zero = jnp.zeros((ROWS, width), F32)
        low = lambda v: jnp.where(row_ids(v) > 0, pltpu.roll(v, 1, 0), 0.0)
        high = lambda v: pltpu.roll(v, ROWS - 1, 0)
        inv_ahead, inv_behind = tile_of(around, (), 0), tile_of(around, (), tiles)
        far_ahead, drv_ahead = tile_of(around, (), 2 * tiles), tile_of(around, (), 2 * tiles + 1)
        far_behind, drv_behind = tile_of(around, (), 2 * tiles + 2), tile_of(around, (), 2 * tiles + 3)

        def get(ref, n):
            return tuple(ref[c, n] for c in range(ref.shape[0]))

        def put(ref, n, values):
            for c, value in enumerate(values):
                ref[c, n] = value

        def own(ref, i):
            return tuple(tile_of(ref, (c, i), 0) for c in range(ref.shape[0]))

        def h_first(i, last):
            here = own(e, i)
            above = tuple(up(e, (c, i), 0, tiles, here[c]) for c in range(2))
            ahead = None if last else (tile_of(e, (1, i + 1), 0), tile_of(e, (2, i + 1), 0))
            new, memory = h_values(here, above, ahead, own(h, i), (psi_h[0, i], psi_h[1, i]), coef_h)
            put(h_one, i + 2, new)
            put(psi_one, i + 2, memory)

        def e_first(i):
            here = get(h_one, i + 2)
            behind = get(h_one, i + 1)[1:]
            curl, _ = curl_of_h(here, (low(here[0]), low(here[1])), behind, (psi_e[0, i], psi_e[1, i]), coef_e)
            values = tuple(tile_of(m, (i,), 0) for m in mats)
            for c in range(3):
                found = material_step(
                    tile_of(e, (c, i), 0), curl[c], tile_of(polar, (c, i), 0), tile_of(current, (c, i), 0), values
                )
                for ref, value in zip((e_one, p_one, c_one), found):
                    ref[c, i + 2] = value

        old = own(e, 0)
        turn = (COURANT * old[2], -COURANT * old[1])
        put(h_one, 1, (zero, *turn))

        def first(i, carry):
            h_first(i, False)
            e_first(i)
            return carry

        lax.fori_loop(0, edge, first, 0)
        h_first(edge, True)
        e_first(edge)
        change, _ = response(*turn, low(turn[0]), COURANT * inv_behind, coef_e[1])
        put(e_one, 1, change)
        out = get(h_one, edge + 2)
        half = COURANT * inv_ahead
        put(e_one, planes + 2, (zero, half * out[2], -half * out[1]))

        def h_second(n, memory, old, ahead):
            here = get(e_one, n)
            new, _ = h_values(here, (high(here[0]), high(here[1])), ahead, old, memory, coef_h)
            put(h_two, n, new)

        def e_second(n, drive, inv, rest):
            hx, hy, hz = get(h_two, n)
            behind = h_two[2, n - 1]
            curl_x = y_backward(hz) - (hy - low(hy))
            curl_y = hx - low(hx) - (hz - behind)
            for c, curl in enumerate((curl_x, curl_y)):
                cur = drive * e_one[c, n]
                if rest is not None:
                    cur = cur + rest[0] * c_one[c, n] - rest[1] * p_one[c, n]
                keep(c, n, e_one[c, n] + inv * (COURANT * curl - cur))

        def keep(c, n, value):
            rows[pl.ds(c * wide + n, 1), :] = value[layers : layers + 1, :]

        rows[...] = jnp.zeros_like(rows)
        put(h_two, 0, (zero, COURANT * e_one[2, 1], -COURANT * e_one[1, 1]))
        h_second(1, (zero, zero), get(h_one, 1), get(e_one, 2)[1:])
        _, hy, hz = get(h_two, 0)
        half = COURANT * far_behind
        keep(0, 0, half * (y_backward(hz) - (hy - low(hy))))
        keep(1, 0, -half * hz)
        e_second(1, drv_behind, inv_behind, None)

        def second(n, carry):
            h_second(n, get(psi_one, n), get(h_one, n), get(e_one, n + 1)[1:])
            inv, dec, drv, spr = (tile_of(m, (n - 2,), 0) for m in mats)
            e_second(n, drv, inv, (dec, spr))
            return carry

        lax.fori_loop(2, planes + 2, second, 0)
        n = planes + 2
        h_second(n, (zero, zero), (zero, zero, zero), None)
        e_second(n, drv_ahead, inv_ahead, None)
        keep(1, n + 1, COURANT * far_ahead * h_two[2, n])
        mixed[...] = jnp.dot(rows[...], table[...], precision=lax.Precision.HIGHEST, preferred_element_type=F32)

    shape = pltpu.VMEM((3, wide, ROWS, width), F32)
    found = pl.pallas_call(
        body,
        name="foretold",
        out_shape=(*state_shapes(planes, depth, width), pltpu.VMEM((count, table.shape[1]), F32)),
        in_specs=[VMEM] * 12,
        out_specs=(VMEM,) * 7,
        input_output_aliases={n: n for n in range(6)},
        scratch_shapes=[
            shape,
            shape,
            shape,
            shape,
            pltpu.VMEM((2, wide, ROWS, width), F32),
            shape,
            pltpu.VMEM((count, width), F32),
        ],
        compiler_params=params(),
    )(*state, *mats, around, table)
    return found[:6], found[6]


def finish(state, mats, back, near, far, around, layers):
    planes, depth, width = state[0].shape[1:]
    tiles = depth // ROWS

    def body(*refs):
        mats, back, near_in, far_in, around = refs[6:10], refs[10], refs[11], refs[12], refs[13]
        state, outs = refs[14:20], refs[20:26]
        ahead, behind = refs[26:28]
        scratch, sem, sem_psi = refs[28:31], refs[31], refs[32]
        coef_h = pml(layers, 0.5, width)
        coef_e = pml(layers, 0.0, width)
        sort_in(near_in, far_in, ahead, behind)
        close_step(state, mats, back, ahead, behind, around, scratch, planes, tiles, coef_h, coef_e)

        def copies(i):
            found = [pltpu.make_async_copy(state[n].at[:, i], outs[n].at[:, i], sem.at[n, i]) for n in range(4)]
            for n in range(2):
                for c in range(2):
                    source = state[4 + n].at[c, i, 0:layers]
                    target = outs[4 + n].at[i, :, c]
                    found.append(pltpu.make_async_copy(source, target, sem_psi.at[2 * n + c, i]))
            return found

        full_step(
            state,
            mats,
            planes,
            tiles,
            coef_h,
            coef_e,
            pair_of(scratch[0], 0, tiles),
            pair_of(scratch[1], 0, tiles),
            after=lambda i: start_all(copies(i)),
        )
        for i in range(planes):
            wait_all(copies(i))

    field = jax.ShapeDtypeStruct((3, planes, depth, width), F32)
    memory = jax.ShapeDtypeStruct((planes, layers, 2, width), F32)
    whole = pltpu.VMEM(near.shape, F32)
    found = pl.pallas_call(
        body,
        name="finish",
        out_shape=(*state_shapes(planes, depth, width), field, field, field, field, memory, memory),
        in_specs=[VMEM] * 14,
        out_specs=(VMEM,) * 6 + (HBM,) * 6,
        input_output_aliases={n: n for n in range(6)},
        scratch_shapes=[
            whole,
            whole,
            *close_scratch(depth, width),
            pltpu.SemaphoreType.DMA((4, planes)),
            pltpu.SemaphoreType.DMA((4, planes)),
        ],
        compiler_params=params(),
    )(*state, *mats, back, near, far, around)
    return found[6:]


def y_table(cells):
    phase = np.arange(cells)[:, None] * (np.arange(KSPAN) - KSPAN // 2)[None, :] % cells
    phase = phase.astype(np.float64) * (2.0 * math.pi / cells)
    return np.concatenate([np.cos(phase), np.sin(phase)], axis=1).astype(np.float32)


def x_table(planes, count):
    rows = spectral_rows(planes)
    cells = planes * count
    wide = planes + 4
    comp = np.full(rows, -1)
    shift = np.zeros(rows, np.int64)
    for c in range(2):
        comp[c * wide : (c + 1) * wide] = c
        shift[c * wide : (c + 1) * wide] = np.arange(wide) - 2
    x = (np.arange(count)[:, None] * planes + shift[None, :]) % cells
    waves = np.arange(KSPAN) - KSPAN // 2
    phase = (waves[:, None, None] * x[None] % cells).astype(np.float64) * (2.0 * math.pi / cells)
    parts = []
    for c in range(2):
        for wave in (np.cos(phase), np.sin(phase)):
            parts.append(np.where(comp[None, None, :] == c, wave, 0.0).reshape(KSPAN, count * rows))
    return np.concatenate(parts, axis=0).astype(np.float32)


def packed(pieces):
    rows, width = pieces[0].shape

    def body(*refs):
        for n in range(len(pieces)):
            refs[-1][n * rows : n * rows + rows, :] = refs[n][...]

    return pl.pallas_call(
        body,
        name="packed",
        out_shape=pltpu.VMEM((rows * len(pieces), width), F32),
        in_specs=[VMEM] * len(pieces),
        out_specs=VMEM,
        compiler_params=params(),
    )(*pieces)


def gathered(block):
    count = lax.axis_size("gx")
    assert count & (count - 1) == 0
    pieces = [block]
    reach = 1
    while reach < count:
        ways = min(4, count // reach)
        held = pieces[0] if len(pieces) == 1 else packed(pieces)
        pieces = [held] + [swapped(held, reach * way) for way in range(1, ways)]
        reach *= ways
    return pieces


def prepared(orders, table_y, table_x):
    wide = orders.shape[1]
    chunk = 512 if wide % 512 == 0 else wide

    def body(orders_in, y_in, x_in, hit_y, hit_x, table_y, table_x, orders, sem):
        wanted = [(orders_in, orders), (y_in, table_y), (x_in, table_x)]
        copies = [pltpu.make_async_copy(s, d, sem.at[n]) for n, (s, d) in enumerate(wanted)]
        start_all(copies)
        wait_all(copies)
        for n in range(wide // chunk):
            span = slice(n * chunk, n * chunk + chunk)
            waves = lax.broadcasted_iota(jnp.int32, (KSPAN, chunk), 0) - KSPAN // 2
            hit = jnp.where(waves == orders[1:2, span], 1.0, 0.0).astype(jnp.bfloat16)
            for part in range(3):
                hit_y[part * KSPAN : (part + 1) * KSPAN, span] = hit
            hit_x[:, span] = jnp.where(waves == orders[0:1, span], 1.0, 0.0)

    return pl.pallas_call(
        body,
        name="prepared",
        out_shape=(
            pltpu.VMEM((3 * KSPAN, wide), jnp.bfloat16),
            pltpu.VMEM((KSPAN, wide), F32),
            pltpu.VMEM(table_y.shape, F32),
            pltpu.VMEM(table_x.shape, F32),
        ),
        in_specs=[HBM] * 3,
        out_specs=(VMEM,) * 4,
        scratch_shapes=[pltpu.VMEM(orders.shape, jnp.int32), pltpu.SemaphoreType.DMA((3,))],
        compiler_params=params(),
    )(in_hbm(orders), in_hbm(table_y), in_hbm(table_x))


def pick_orders(pieces, table, hit_y, hit_x, cells_total):
    count = lax.axis_size("gx")
    total = sum(piece.shape[0] for piece in pieces)
    rows = total // count
    wide = hit_x.shape[1]
    chunk = 512 if wide % 512 == 0 else wide
    scale = 1.0 / math.sqrt(cells_total)

    def body(*refs):
        held = refs[: len(pieces)]
        table, hit_y, hit_x, out, mixed = refs[len(pieces) :]
        here = lax.axis_index("gx")
        at = 0
        for ref in held:
            for n in range(ref.shape[0] // rows):
                slot = jnp.bitwise_xor(here, at)
                mixed[pl.ds(pl.multiple_of(slot * rows, rows), rows), :] = ref[n * rows : n * rows + rows, :]
                at += 1
        both = jnp.dot(table[...], mixed[...], precision=lax.Precision.HIGHEST, preferred_element_type=F32)
        parts = []
        for c in range(2):
            cosine = both[2 * c * KSPAN : (2 * c + 1) * KSPAN]
            sine = both[(2 * c + 1) * KSPAN : (2 * c + 2) * KSPAN]
            parts.append((cosine[:, :KSPAN] - sine[:, KSPAN:]) * scale)
            parts.append((cosine[:, KSPAN:] + sine[:, :KSPAN]) * -scale)
        spectrum = jnp.concatenate(parts, axis=0)
        high = spectrum.astype(jnp.bfloat16)
        rest = spectrum - high.astype(F32)
        mid = rest.astype(jnp.bfloat16)
        low = (rest - mid.astype(F32)).astype(jnp.bfloat16)
        split = jnp.concatenate([high, mid, low], axis=1)
        for n in range(wide // chunk):
            span = slice(n * chunk, n * chunk + chunk)
            lines = jnp.dot(split, hit_y[:, span], preferred_element_type=F32)
            hit = hit_x[:, span]
            for q in range(4):
                line = lines[q * KSPAN : (q + 1) * KSPAN] * hit
                out[q : q + 1, span] = jnp.sum(line, axis=0, keepdims=True)

    return pl.pallas_call(
        body,
        name="pick_orders",
        out_shape=jax.ShapeDtypeStruct((4, wide), F32),
        in_specs=[VMEM] * (len(pieces) + 3),
        out_specs=VMEM,
        scratch_shapes=[pltpu.VMEM((total, 2 * KSPAN), F32)],
        compiler_params=params(),
    )(*pieces, table, hit_y, hit_x)


def shards(
    e_field,
    h_field,
    polar,
    current,
    psi_h,
    psi_e,
    material,
    inv_eps_table,
    decay_table,
    drive_table,
    strength_table,
    spring_table,
    orders,
):
    planes, _, width = material.shape
    layers = psi_h.shape[2]
    count = lax.axis_size("gx")
    tables = (inv_eps_table, decay_table, drive_table, strength_table, spring_table)
    memories = tuple(jnp.transpose(psi, (1, 2, 0, 3)) for psi in (psi_h, psi_e))

    state, kinds, mats, near, far, back = begin(
        (e_field, h_field, polar, current), memories, material, tables
    )
    near, far = exchanged(near, far)
    state, mats = interior(state, mats, layers, kinds, tables)
    hit_y, hit_x, table_y, table_x = prepared(orders, jnp.asarray(y_table(width)), jnp.asarray(x_table(planes, count)))
    state, near, far, back, around = middle(state, mats, back, near, far, layers)
    near, far = exchanged(near, far)
    state, mixed = foretold(state, mats, around, table_y, layers)
    state, _ = interior(state, mats, layers)
    pieces = gathered(mixed)
    outs = finish(state, mats, back, near, far, around, layers)
    pupil = pick_orders(pieces, table_x, hit_y, hit_x, planes * count * width)
    outs = (*outs[:4], *(jnp.transpose(psi, (2, 0, 1, 3)) for psi in outs[4:]))
    return (*outs, pupil)


def solution(mesh):
    split = P(None, ("mask", "gx"), None, None)
    in_specs = (split,) * 6 + (P(("mask", "gx"), None, None),) + (P(),) * 6
    out_specs = (split,) * 6 + (P(None, "mask"),)
    return jax.shard_map(shards, mesh=mesh, in_specs=in_specs, out_specs=out_specs, check_vma=False)
```
